32 devices in a mesh: owner: 8 (over z, core), dp: 4 (over y, x).
Axes of the slice: x: 2, y: 2, z: 4, core: 2. Of those that a mesh axis runs over, the one named last changes fastest.
Arguments:
- tokens: bfloat16 [1536, 2048], P(('owner', 'dp')), may hold values from -6 to 6
- upstream: bfloat16 [1536, 2048], P(('owner', 'dp')), may hold values from -6 to 6
- lang_ids: int32 [1536], P(('owner', 'dp')), may hold values from 0 to 7, as said below
- up_weight: bfloat16 [8, 2048, 4096], P('owner', None, 'dp'), may hold values from -0.125 to 0.125
- down_weight: bfloat16 [8, 4096, 2048], P('owner', 'dp'), may hold values from -0.09375 to 0.09375
Outputs:
- input_grad: bfloat16 [1536, 2048], P(('owner', 'dp'))
- grad_up: bfloat16 [8, 2048, 4096], P('owner', None, 'dp')
- grad_down: bfloat16 [8, 4096, 2048], P('owner', 'dp')
The draws below stay inside these ranges and needn't reach their ends.
Inputs may be any that keep to these rules, and one draw needn't show every extreme that they name: `lang_ids`: within the tokens of one device (each aligned block of 48 tokens) no language occurs more than 8 times, and one language occurs exactly 8 times in every such block.
All inputs are finite; a program needn't handle non-finite values.
Results may differ from the reference program's by a relative error of at most 0.007.
Values may be sent and summed in bfloat16 or wider, within the bound.
A program may use at most 64 MiB of HBM per device.

```python
import jax
import jax.numpy as jnp
from jax import lax

D = 2048
H = 4096
TOK_DEV = 48
LANGS = 8
CAP = 8
TOKENS = 1536
ROWS_LANG = 192
N_DP = 4


def draw_lang_ids(key, part):
    block_count = TOKENS // TOK_DEV
    hot_lang = jax.random.randint(jax.random.fold_in(key, 7), (), 0, LANGS)
    pair_lang = (jnp.arange(LANGS * CAP, dtype=jnp.int32) // CAP).astype(jnp.int32)

    def one_block(block_index):
        block_key = jax.random.fold_in(key, block_index + 11)
        scores = jax.random.permutation(block_key, LANGS * CAP).astype(jnp.int32) + 1
        scores = jnp.where(pair_lang == hot_lang, 0, scores)
        order = jnp.argsort(scores, stable=True)
        chosen = pair_lang[order[:TOK_DEV]]
        placing = jax.random.permutation(jax.random.fold_in(block_key, 3), TOK_DEV)
        return chosen[placing]
    blocks = jax.vmap(one_block)(jnp.arange(block_count, dtype=jnp.int32))
    return blocks.reshape(TOKENS).astype(jnp.int32)


def level_of(key, extent, cuts, low, top_value):
    factor_of, own = 1.0, jax.random.fold_in(key, 6)
    for axis_at, shards_of in cuts:
        heights = jnp.exp(jax.random.uniform(jax.random.fold_in(own, axis_at), (shards_of,), jnp.float32, low / len(cuts), top_value / len(cuts)))
        factor_of = factor_of * jnp.repeat(heights, extent[axis_at] // shards_of).reshape([-1 if axis == axis_at else 1 for axis in range(len(extent))])
    return factor_of


def bell_draw(own_key, extent, width, limit, pieces=(), kind=jnp.bfloat16):
    result = jax.random.normal(own_key, extent, jnp.float32) * width
    if len(pieces) > 0:
        result = level_of(own_key, extent, pieces, -0.22, 0.18) * result
    return jnp.clip(result, min=-limit, max=limit).astype(kind)


def setup_inputs(seed: int = 0) -> dict:
    key_list = jax.random.split(jax.random.key(seed), 6)
    tokens = bell_draw(key_list[0], (TOKENS, D), 1.0, 6.0, ((0, 32),))
    upstream = bell_draw(key_list[1], (TOKENS, D), 1.0, 6.0, ((0, 32),))
    lang_ids = draw_lang_ids(jax.random.fold_in(key_list[5], 71), 0)
    up_weight = bell_draw(key_list[3], (LANGS, D, H), D ** -0.5, 0.125, ((0, 8), (2, 4)))
    down_weight = bell_draw(key_list[4], (LANGS, H, D), H ** -0.5, 0.09375, ((0, 8), (1, 4)))
    return {"tokens": tokens, "upstream": upstream, "lang_ids": lang_ids, "up_weight": up_weight, "down_weight": down_weight}


def reference(tokens, upstream, lang_ids, up_weight, down_weight):
    device_count = TOKENS // TOK_DEV
    block_ids = lang_ids.reshape(device_count, TOK_DEV)
    matches = block_ids[:, :, None] == block_ids[:, None, :]
    positions = jnp.arange(TOK_DEV, dtype=jnp.int32)
    earlier = positions[None, :] < positions[:, None]
    slots = lax.optimization_barrier(jnp.sum(jnp.logical_and(matches, earlier[None]), axis=2)).astype(jnp.int32)
    table_rows = (jnp.arange(device_count, dtype=jnp.int32)[:, None] * CAP + slots).reshape(-1).astype(jnp.int32)
    table = jnp.full((LANGS, device_count * CAP), TOKENS, jnp.int32)
    table = table.at[lang_ids, table_rows].set(jnp.arange(TOKENS, dtype=jnp.int32))
    zero_row = jnp.zeros((1, D), tokens.dtype)
    padded_inputs = jnp.concatenate([tokens, zero_row], axis=0)
    padded_upstream = jnp.concatenate([upstream, zero_row], axis=0)
    grad_scale = float(ROWS_LANG) ** (-0.5)
    block_width = H // N_DP

    def per_language(carry_sum, inputs):
        index_rows, up_matrix, down_matrix = inputs
        row_inputs = padded_inputs[index_rows]
        row_upstream = padded_upstream[index_rows]
        pre_act = jnp.dot(row_inputs, up_matrix, preferred_element_type=jnp.float32)
        activated, pullback = jax.vjp(jax.nn.gelu, pre_act)
        hidden = activated.astype(jnp.bfloat16)
        hidden_grad = jnp.dot(row_upstream, down_matrix.T, preferred_element_type=jnp.float32)
        pre_grad = pullback(hidden_grad)[0].astype(jnp.bfloat16)
        grad_up = (jnp.dot(row_inputs.T, pre_grad, preferred_element_type=jnp.float32) * grad_scale).astype(jnp.bfloat16)
        grad_down = (jnp.dot(hidden.T, row_upstream, preferred_element_type=jnp.float32) * grad_scale).astype(jnp.bfloat16)
        row_total = index_rows.shape[0]
        partial_value = jnp.einsum('rkh,dkh->krd', pre_grad.astype(jnp.float32).reshape(row_total, N_DP, block_width), up_matrix.astype(jnp.float32).reshape(D, N_DP, block_width), precision=lax.Precision.HIGHEST)
        rounded = lax.optimization_barrier(partial_value.astype(jnp.bfloat16))
        adapter_grad = lax.optimization_barrier(jnp.sum(rounded.astype(jnp.float32), axis=0)).astype(jnp.bfloat16)
        adapter_grad = lax.optimization_barrier(adapter_grad)
        carry_sum = carry_sum.at[index_rows].add(adapter_grad.astype(jnp.float32))
        return (carry_sum, (grad_up, grad_down))
    start_sum = jnp.zeros((TOKENS + 1, D), jnp.float32)
    total_sum, grads = lax.scan(per_language, start_sum, (table, up_weight, down_weight))
    input_grad = (upstream.astype(jnp.float32) + total_sum[:TOKENS]).astype(jnp.bfloat16)
    return (input_grad, grads[0], grads[1])
```

```python
import functools

import jax
import jax.numpy as jnp
from jax import lax
from jax.experimental import pallas as pl
from jax.experimental.pallas import tpu as pltpu
from jax.sharding import PartitionSpec as P

MESH = pl.DeviceIdType.MESH


def partner(index, step, count):
    total, bit = 0, 1
    while bit < count:
        digit = (index // bit) % 2
        total = total + bit * ((1 - digit) if (step // bit) % 2 else digit)
        bit *= 2
    return total


def greet(me_owner, me_group, owners, groups):
    barrier = pltpu.get_barrier_semaphore()
    for step in range(1, owners):
        pl.semaphore_signal(
            barrier, inc=1, device_id=(partner(me_owner, step, owners), me_group), device_id_type=MESH
        )
    for step in range(1, groups):
        pl.semaphore_signal(
            barrier, inc=1, device_id=(me_owner, partner(me_group, step, groups)), device_id_type=MESH
        )


def enter(me_owner, me_group, owners, groups):
    greet(me_owner, me_group, owners, groups)
    pl.semaphore_wait(pltpu.get_barrier_semaphore(), owners + groups - 2)


def spread_kernel(owners, groups, pieces, *refs):
    sources, dests = refs[0:2], refs[2:4]
    a_send, a_recv, b_send, b_recv, c_send, c_recv = refs[4:]
    me_owner, me_group = lax.axis_index("owner"), lax.axis_index("dp")
    per_piece = owners // pieces
    relay = groups == 4
    direct = [1, 2] if relay else list(range(1, groups))
    enter(me_owner, me_group, owners, groups)
    sends = []

    for step in range(1, owners):
        peer = partner(me_owner, step, owners)
        for which in range(2):
            copy = pltpu.make_async_remote_copy(
                src_ref=sources[which].at[peer],
                dst_ref=dests[which].at[me_group, me_owner],
                send_sem=a_send.at[which, step],
                recv_sem=a_recv.at[which, step],
                device_id=(peer, me_group),
                device_id_type=MESH,
            )
            copy.start()
            sends.append(copy)
    for which in range(2):
        dests[which][me_group, me_owner] = sources[which][me_owner]

    def piece_of(group, piece):
        here = partner(me_owner // per_piece, piece, pieces) * per_piece
        return group, pl.ds(here, per_piece)

    def hop(which, group, piece, step, send_sem, recv_sem):
        group_at, rows_at = piece_of(group, piece)
        return pltpu.make_async_remote_copy(
            src_ref=dests[which].at[group_at, rows_at],
            dst_ref=dests[which].at[group_at, rows_at],
            send_sem=send_sem,
            recv_sem=recv_sem,
            device_id=(me_owner, partner(me_group, step, groups)),
            device_id_type=MESH,
        )

    def forward(piece):
        for which in range(2):
            near, far = (1, 2) if which == 0 else (2, 1)
            group = partner(me_group, near, groups)
            hop(which, group, piece, near, b_send.at[which, near, piece], b_recv.at[which, near, piece]).wait_recv()
            copy = hop(which, group, piece, far, c_send.at[which, piece], c_recv.at[which, piece])
            copy.start()
            sends.append(copy)

    for piece in range(pieces):
        for inner in range(per_piece):
            step = piece * per_piece + inner
            if step == 0:
                continue
            peer = partner(me_owner, step, owners)
            for which in range(2):
                pltpu.make_async_remote_copy(
                    src_ref=sources[which].at[peer],
                    dst_ref=dests[which].at[me_group, peer],
                    send_sem=a_send.at[which, step],
                    recv_sem=a_recv.at[which, step],
                    device_id=(peer, me_group),
                    device_id_type=MESH,
                ).wait_recv()
        for step in direct:
            for which in range(2):
                copy = hop(which, me_group, piece, step, b_send.at[which, step, piece], b_recv.at[which, step, piece])
                copy.start()
                sends.append(copy)
        if relay and piece >= 1:
            forward(piece - 1)
    if relay:
        forward(pieces - 1)
    for piece in range(pieces):
        for which in range(2):
            for step in direct:
                if relay and step == (1 if which == 0 else 2):
                    continue
                group = partner(me_group, step, groups)
                hop(which, group, piece, step, b_send.at[which, step, piece], b_recv.at[which, step, piece]).wait_recv()
            if relay:
                group = partner(me_group, 3, groups)
                hop(which, group, piece, 1 if which else 2, c_send.at[which, piece], c_recv.at[which, piece]).wait_recv()
    for copy in sends:
        copy.wait_send()


def collect_kernel(owners, groups, pieces, parts, back, landed, summed, b_send, b_recv, a_send, a_recv):
    me_owner, me_group = lax.axis_index("owner"), lax.axis_index("dp")
    per_piece = owners // pieces
    enter(me_owner, me_group, owners, groups)
    sends = []

    def share(piece, step):
        here = pl.ds(partner(me_owner // per_piece, piece, pieces) * per_piece, per_piece)
        peer = partner(me_group, step, groups)
        return pltpu.make_async_remote_copy(
            src_ref=parts.at[peer, here],
            dst_ref=landed.at[step - 1, here],
            send_sem=b_send.at[step, piece],
            recv_sem=b_recv.at[step, piece],
            device_id=(me_owner, peer),
            device_id_type=MESH,
        )

    order = list(range(pieces))[::-1]
    for piece in order:
        for step in list(range(1, groups))[::-1]:
            copy = share(piece, step)
            copy.start()
            sends.append(copy)

    def ship(step):
        peer = partner(me_owner, step, owners)
        return pltpu.make_async_remote_copy(
            src_ref=summed.at[peer],
            dst_ref=back.at[me_owner],
            send_sem=a_send.at[step],
            recv_sem=a_recv.at[step],
            device_id=(peer, me_group),
            device_id_type=MESH,
        )

    for piece in order:
        for step in range(1, groups):
            share(piece, step).wait_recv()
        for inner in range(per_piece):
            step = piece * per_piece + inner
            peer = partner(me_owner, step, owners)
            total = parts[me_group, peer].astype(jnp.float32)
            for other in range(1, groups):
                total = total + landed[other - 1, peer].astype(jnp.float32)
            rounded = total.astype(jnp.bfloat16)
            if step == 0:
                back[peer] = rounded
            else:
                summed[peer] = rounded
                copy = ship(step)
                copy.start()
                sends.append(copy)
    for step in range(1, owners):
        peer = partner(me_owner, step, owners)
        pltpu.make_async_remote_copy(
            src_ref=summed.at[peer],
            dst_ref=back.at[peer],
            send_sem=a_send.at[step],
            recv_sem=a_recv.at[step],
            device_id=(peer, me_group),
            device_id_type=MESH,
        ).wait_recv()
    for copy in sends:
        copy.wait_send()


def spread(send_inputs, send_upstream, owners, groups):
    _, slots, width = send_inputs.shape
    pieces = owners // 2 if groups == 4 else 1
    whole = jax.ShapeDtypeStruct((groups, owners, slots, width), jnp.bfloat16)
    vmem = pl.BlockSpec(memory_space=pltpu.VMEM)
    dma = pltpu.SemaphoreType.DMA
    return pl.pallas_call(
        functools.partial(spread_kernel, owners, groups, pieces),
        out_shape=(whole, whole),
        in_specs=[vmem, vmem],
        out_specs=(vmem, vmem),
        scratch_shapes=[
            dma((2, owners)),
            dma((2, owners)),
            dma((2, groups, pieces)),
            dma((2, groups, pieces)),
            dma((2, pieces)),
            dma((2, pieces)),
        ],
        compiler_params=pltpu.CompilerParams(
            collective_id=0, has_side_effects=True, vmem_limit_bytes=24 << 20
        ),
    )(send_inputs, send_upstream)


def collect(parts, owners, groups):
    _, _, slots, width = parts.shape
    pieces = owners // 2 if groups == 4 else 1
    vmem = pl.BlockSpec(memory_space=pltpu.VMEM)
    dma = pltpu.SemaphoreType.DMA
    return pl.pallas_call(
        functools.partial(collect_kernel, owners, groups, pieces),
        out_shape=jax.ShapeDtypeStruct((owners, slots, width), jnp.bfloat16),
        in_specs=[vmem],
        out_specs=vmem,
        scratch_shapes=[
            pltpu.VMEM((groups - 1, owners, slots, width), jnp.bfloat16),
            pltpu.VMEM((owners, slots, width), jnp.bfloat16),
            dma((groups, pieces)),
            dma((groups, pieces)),
            dma((owners,)),
            dma((owners,)),
        ],
        compiler_params=pltpu.CompilerParams(
            collective_id=1, has_side_effects=True, vmem_limit_bytes=24 << 20
        ),
    )(parts)


def fused_kernel(owners, pieces, scale, *refs):
    (ids, tokens, upstream, up_hbm, down_hbm), refs = refs[0:5], refs[5:]
    (input_grad, grad_up, grad_down), refs = refs[0:3], refs[3:]
    rows, (hidden, pre_grad), refs = refs[0:2], refs[2:4], refs[4:]
    back, refs = refs[0], refs[1:]
    sources, dests, (up, down, parts, landed, summed), refs = refs[0:2], refs[2:4], refs[4:9], refs[9:]
    w_sem, a_send, a_recv, b_send, b_recv, c_send, c_recv, d_send, d_recv, e_send, e_recv = refs
    arrivals = (tokens, upstream)
    groups = 4
    slots, width = sources[0].shape[1:]
    units = up.shape[1]
    step_rows = groups * slots
    unit_tile, wide = units // 2, width // 2
    me_owner, me_group = lax.axis_index("owner"), lax.axis_index("dp")
    greet(me_owner, me_group, owners, groups)
    weight_copies = [
        pltpu.make_async_copy(up_hbm, up, w_sem.at[0]),
        pltpu.make_async_copy(down_hbm, down, w_sem.at[1]),
    ]
    for copy in weight_copies:
        copy.start()
    tok_count = ids.shape[1]
    row_ids = ids[...]
    square = (tok_count, tok_count)
    first_at = lax.broadcasted_iota(jnp.int32, square, 0)
    second_at = lax.broadcasted_iota(jnp.int32, square, 1)
    spread_ids = jnp.broadcast_to(row_ids.astype(jnp.float32), square)
    column_ids = jnp.sum(jnp.where(first_at == second_at, spread_ids, 0.0), axis=1, keepdims=True)
    same = jnp.logical_and(column_ids == spread_ids, first_at < second_at)
    ranks = jnp.sum(jnp.where(same, 1.0, 0.0), axis=0, keepdims=True).astype(jnp.int32)
    target = jnp.bitwise_xor(row_ids, me_owner) * slots + ranks
    positions = lax.broadcasted_iota(jnp.int32, (owners * slots, tok_count), 0)
    placer = jnp.where(positions == target, 1.0, 0.0).astype(jnp.bfloat16)
    for which in range(2):
        placed = jnp.dot(placer, arrivals[which][...], preferred_element_type=jnp.float32)
        for step in range(owners):
            block = placed[step * slots : (step + 1) * slots, :].astype(jnp.bfloat16)
            (sources if step else dests)[which][(step,) if step else (0, 0)] = block
    pl.semaphore_wait(pltpu.get_barrier_semaphore(), owners + groups - 2)
    sends = []

    def go(copy):
        copy.start()
        sends.append(copy)

    def along_owner(source, dest, step, send_sem, recv_sem):
        return pltpu.make_async_remote_copy(
            src_ref=source,
            dst_ref=dest,
            send_sem=send_sem,
            recv_sem=recv_sem,
            device_id=(partner(me_owner, step, owners), me_group),
            device_id_type=MESH,
        )

    def along_group(source, dest, step, send_sem, recv_sem):
        return pltpu.make_async_remote_copy(
            src_ref=source,
            dst_ref=dest,
            send_sem=send_sem,
            recv_sem=recv_sem,
            device_id=(me_owner, partner(me_group, step, groups)),
            device_id_type=MESH,
        )

    def out_copy(which, step):
        return along_owner(
            sources[which].at[step], dests[which].at[step, 0], step, a_send.at[which, step], a_recv.at[which, step]
        )

    def near_copy(which, step, side):
        return along_group(
            dests[which].at[step, 0],
            dests[which].at[step, side],
            side,
            b_send.at[which, side, step],
            b_recv.at[which, side, step],
        )

    def relay_copy(which, step):
        first, second = (1, 2) if which == 0 else (2, 1)
        return along_group(
            dests[which].at[step, first],
            dests[which].at[step, 3],
            second,
            c_send.at[which, step],
            c_recv.at[which, step],
        )

    def part_copy(piece, chunk, side):
        here, cols = pl.ds(piece[0], len(piece)), pl.ds(chunk * wide, wide)
        return along_group(
            parts.at[here, side, :, cols],
            landed.at[here, side - 1, :, cols],
            side,
            d_send.at[side, piece[0], chunk],
            d_recv.at[side, piece[0], chunk],
        )

    def back_copy(step, chunk):
        cols = pl.ds(chunk * wide, wide)
        return along_owner(
            summed.at[step, :, cols],
            back.at[step, :, cols],
            step,
            e_send.at[step, chunk],
            e_recv.at[step, chunk],
        )

    def out(*steps):
        for step in steps:
            for which in range(2):
                go(out_copy(which, step))

    def arrive(*steps):
        for step in steps:
            for which in range(2):
                if step:
                    out_copy(which, step).wait_recv()
                for side in (1, 2):
                    go(near_copy(which, step, side))

    def forward(*steps):
        for step in steps:
            for which in range(2):
                near_copy(which, step, 1 if which == 0 else 2).wait_recv()
                go(relay_copy(which, step))

    def gather(piece):
        for step in piece:
            for which in range(2):
                near_copy(which, step, 2 if which == 0 else 1).wait_recv()
                relay_copy(which, step).wait_recv()
        base = piece[0] * step_rows
        for which in range(2):
            rows[which][base : base + len(piece) * step_rows, :] = jnp.concatenate(
                [dests[which][step, group].astype(jnp.float32) for step in piece for group in range(groups)], axis=0
            ).astype(jnp.bfloat16)

    def activate(piece, tile):
        here = pl.ds(piece[0] * step_rows, len(piece) * step_rows)
        cols = pl.ds(tile * unit_tile, unit_tile)
        pre_act = jnp.dot(rows[0][here, :], up[:, cols], preferred_element_type=jnp.float32)
        hidden_grad = lax.dot_general(
            rows[1][here, :], down[cols, :], (((1,), (1,)), ((), ())), preferred_element_type=jnp.float32
        )
        activated, pullback = jax.vjp(jax.nn.gelu, pre_act)
        hidden[here, cols] = activated.astype(jnp.bfloat16)
        pre_grad[here, cols] = pullback(hidden_grad)[0].astype(jnp.bfloat16)

    def project(piece, chunk):
        here = pl.ds(piece[0] * step_rows, len(piece) * step_rows)
        cols = pl.ds(chunk * wide, wide)
        part = lax.dot_general(
            pre_grad[here, :], up[cols, :], (((1,), (1,)), ((), ())), preferred_element_type=jnp.float32
        )
        for at in range(len(piece) * groups):
            step, group = piece[at // groups], at % groups
            parts[step, group, :, cols] = part[at * slots : (at + 1) * slots, :].astype(jnp.bfloat16)
        for side in (3, 1, 2):
            go(part_copy(piece, chunk, side))

    def reduce(piece, chunk):
        cols = pl.ds(chunk * wide, wide)
        for side in (1, 2, 3):
            part_copy(piece, chunk, side).wait_recv()
        for step in piece[::-1]:
            total = parts[step, 0, :, cols].astype(jnp.float32)
            for other in range(groups - 1):
                total = total + landed[step, other, :, cols].astype(jnp.float32)
            rounded = total.astype(jnp.bfloat16)
            if step == 0:
                back[0, :, cols] = rounded
            else:
                summed[step, :, cols] = rounded
                go(back_copy(step, chunk))

    def weight_grad(left, right, out):
        tile = 512

        def one(index, carry):
            cols = pl.ds(pl.multiple_of(index * tile, tile), tile)
            term = lax.dot_general(
                left[:, cols], right[...], (((0,), (0,)), ((), ())), preferred_element_type=jnp.float32
            )
            out[cols, :] = (term * scale).astype(jnp.bfloat16)
            return carry

        lax.fori_loop(0, left.shape[1] // tile, one, 0)

    first, second, third = pieces
    out(1, 4, 5)
    arrive(0)
    out(2, 3)
    arrive(1)
    forward(0)
    forward(1)
    arrive(2, 3)
    out(6, 7)
    for copy in weight_copies:
        copy.wait()
    gather(first)
    activate(first, 0)
    arrive(4, 5)
    forward(2, 3)
    activate(first, 1)
    arrive(6, 7)
    forward(4, 5)
    project(first, 0)
    project(first, 1)
    gather(second)
    activate(second, 0)
    forward(6, 7)
    activate(second, 1)
    project(second, 0)
    project(second, 1)
    gather(third)
    activate(third, 0)
    activate(third, 1)
    project(third, 0)
    project(third, 1)
    reduce(first, 0)
    reduce(first, 1)
    reduce(second, 0)
    reduce(second, 1)
    weight_grad(rows[0], pre_grad, grad_up)
    reduce(third, 0)
    reduce(third, 1)
    weight_grad(hidden, rows[1], grad_down)
    for step in range(1, owners):
        for chunk in range(2):
            back_copy(step, chunk).wait_recv()
    returned = jnp.concatenate([back[step].astype(jnp.float32) for step in range(owners)], axis=0)
    adapter_grad = lax.dot_general(
        placer, returned.astype(jnp.bfloat16), (((0,), (0,)), ((), ())), preferred_element_type=jnp.float32
    )
    input_grad[...] = (upstream[...].astype(jnp.float32) + adapter_grad).astype(jnp.bfloat16)
    for copy in sends:
        copy.wait_send()


def fused(lang_ids, tokens, upstream, up_matrix, down_matrix, scale, owners, slots):
    width = tokens.shape[1]
    units = up_matrix.shape[1]
    groups = 4
    pieces = ((0, 1), (2, 3, 4, 5), (6, 7))
    total = owners * groups * slots
    vmem = pl.BlockSpec(memory_space=pltpu.VMEM)
    anywhere = pl.BlockSpec(memory_space=pltpu.HBM)
    dma = pltpu.SemaphoreType.DMA
    bf16 = jnp.bfloat16
    grid = (owners, groups, slots, width)
    held = [((total, width), bf16), ((total, width), bf16), ((total, units), bf16), ((total, units), bf16)]
    outs = [(tokens.shape, bf16), ((width, units), bf16), ((units, width), bf16)]
    return pl.pallas_call(
        functools.partial(fused_kernel, owners, pieces, scale),
        out_shape=[jax.ShapeDtypeStruct(*item) for item in outs],
        in_specs=[vmem] * 3 + [anywhere] * 2,
        out_specs=[vmem] * len(outs),
        scratch_shapes=[pltpu.VMEM(*item) for item in held]
        + [
            pltpu.VMEM((owners, slots, width), bf16),
            pltpu.VMEM((owners, slots, width), bf16),
            pltpu.VMEM((owners, slots, width), bf16),
            pltpu.VMEM(grid, bf16),
            pltpu.VMEM(grid, bf16),
            pltpu.VMEM((width, units), bf16),
            pltpu.VMEM((units, width), bf16),
            pltpu.VMEM(grid, bf16),
            pltpu.VMEM((owners, groups - 1, slots, width), bf16),
            pltpu.VMEM((owners, slots, width), bf16),
            dma((2,)),
            dma((2, owners)),
            dma((2, owners)),
            dma((2, groups, owners)),
            dma((2, groups, owners)),
            dma((2, owners)),
            dma((2, owners)),
            dma((groups, owners, 2)),
            dma((groups, owners, 2)),
            dma((owners, 2)),
            dma((owners, 2)),
        ],
        compiler_params=pltpu.CompilerParams(
            collective_id=2, has_side_effects=True, vmem_limit_bytes=44 << 20
        ),
    )(lang_ids[None], tokens, upstream, up_matrix, down_matrix)


def publish_kernel(count, splits, *refs):
    sources, dests, sem = refs[:count], refs[count : 2 * count], refs[2 * count]
    copies = []
    for at, (source, dest) in enumerate(zip(sources, dests)):
        rows = source.shape[0] // splits[at]
        for part in range(splits[at]):
            here = pl.ds(part * rows, rows)
            copies.append(
                pltpu.make_async_copy(source.at[here], dest.at[here], sem.at[sum(splits[:at]) + part])
            )
    for copy in copies:
        copy.start()
    for copy in copies:
        copy.wait()


def publish(*arrays):
    splits = [4 if array.shape[0] % 64 == 0 else 1 for array in arrays]
    anywhere = pl.BlockSpec(memory_space=pl.ANY)
    return pl.pallas_call(
        functools.partial(publish_kernel, len(arrays), splits),
        out_shape=[jax.ShapeDtypeStruct(array.shape, array.dtype) for array in arrays],
        in_specs=[pl.BlockSpec(memory_space=pltpu.VMEM)] * len(arrays),
        out_specs=[anywhere] * len(arrays),
        scratch_shapes=[pltpu.SemaphoreType.DMA((sum(splits),))],
        compiler_params=pltpu.CompilerParams(vmem_limit_bytes=16 << 20),
    )(*arrays)


def placement_matrix(block_ids, owners, slot_count):
    tok_count = block_ids.shape[0]
    matches = block_ids[:, None] == block_ids[None, :]
    positions = jnp.arange(tok_count, dtype=jnp.int32)
    earlier = positions[None, :] < positions[:, None]
    slots = jnp.sum(jnp.logical_and(matches, earlier), axis=1)
    target = block_ids * slot_count + slots
    return (target[None, :] == jnp.arange(owners * slot_count, dtype=jnp.int32)[:, None]).astype(
        jnp.bfloat16
    )


def local(tokens, upstream, lang_ids, up_weight, down_weight):
    owners = lax.axis_size("owner")
    groups = lax.axis_size("dp")
    tok_count, width = tokens.shape
    slots = max(2, 4 * tok_count // (3 * owners))
    rows_here = owners * slots
    up_matrix = up_weight[0]
    down_matrix = down_weight[0]
    grad_scale = float(tok_count * groups) ** (-0.5)
    one_kernel = (
        groups == 4
        and slots == 8
        and owners == 8
        and width % 512 == 0
        and up_matrix.shape[1] % 512 == 0
    )
    if one_kernel:
        input_grad, grad_up, grad_down = fused(
            lang_ids, tokens, upstream, up_matrix, down_matrix, grad_scale, owners, slots
        )
        input_grad, grad_up, grad_down = publish(input_grad, grad_up, grad_down)
        return (input_grad, grad_up[None], grad_down[None])
    placer = placement_matrix(lang_ids, owners, slots)
    send_inputs = jnp.dot(placer, tokens, preferred_element_type=jnp.float32).astype(jnp.bfloat16)
    send_upstream = jnp.dot(placer, upstream, preferred_element_type=jnp.float32).astype(jnp.bfloat16)
    send_inputs = send_inputs.reshape(owners, slots, width)
    send_upstream = send_upstream.reshape(owners, slots, width)
    row_inputs, row_upstream = spread(
        send_inputs,
        send_upstream,
        owners,
        groups,
    )
    row_inputs = row_inputs.reshape(groups * rows_here, width)
    row_upstream = row_upstream.reshape(groups * rows_here, width)
    pre_act = jnp.dot(row_inputs, up_matrix, preferred_element_type=jnp.float32)
    activated, pullback = jax.vjp(jax.nn.gelu, pre_act)
    hidden = activated.astype(jnp.bfloat16)
    hidden_grad = lax.dot_general(
        row_upstream, down_matrix, (((1,), (1,)), ((), ())), preferred_element_type=jnp.float32
    )
    pre_grad = pullback(hidden_grad)[0].astype(jnp.bfloat16)
    parts = lax.dot_general(
        pre_grad, up_matrix, (((1,), (1,)), ((), ())), preferred_element_type=jnp.float32
    ).astype(jnp.bfloat16)
    returned = collect(parts.reshape(groups, owners, slots, width), owners, groups)
    up_term = lax.dot_general(
        row_inputs, pre_grad, (((0,), (0,)), ((), ())), preferred_element_type=jnp.float32
    )
    down_term = lax.dot_general(
        hidden, row_upstream, (((0,), (0,)), ((), ())), preferred_element_type=jnp.float32
    )
    grad_up = (up_term * grad_scale).astype(jnp.bfloat16)
    grad_down = (down_term * grad_scale).astype(jnp.bfloat16)
    adapter_grad = lax.dot_general(
        placer,
        returned.reshape(rows_here, width),
        (((0,), (0,)), ((), ())),
        preferred_element_type=jnp.float32,
    )
    input_grad = (upstream.astype(jnp.float32) + adapter_grad).astype(jnp.bfloat16)
    return (input_grad, grad_up[None], grad_down[None])


def solution(mesh):
    in_specs = (
        P(("owner", "dp"), None),
        P(("owner", "dp"), None),
        P(("owner", "dp")),
        P("owner", None, "dp"),
        P("owner", "dp", None),
    )
    out_specs = (P(("owner", "dp"), None), P("owner", None, "dp"), P("owner", "dp", None))
    return jax.shard_map(local, mesh=mesh, in_specs=in_specs, out_specs=out_specs, check_vma=False)
```

```python
import functools

import jax
import jax.numpy as jnp
from jax import lax
from jax.experimental import pallas as pl
from jax.experimental.pallas import tpu as pltpu
from jax.sharding import PartitionSpec as P

MESH = pl.DeviceIdType.MESH


def partner(index, step, count):
    total, bit = 0, 1
    while bit < count:
        digit = (index // bit) % 2
        total = total + bit * ((1 - digit) if (step // bit) % 2 else digit)
        bit *= 2
    return total


def greet(me_owner, me_group, owners, groups):
    barrier = pltpu.get_barrier_semaphore()
    for step in range(1, owners):
        pl.semaphore_signal(
            barrier, inc=1, device_id=(partner(me_owner, step, owners), me_group), device_id_type=MESH
        )
    for step in range(1, groups):
        pl.semaphore_signal(
            barrier, inc=1, device_id=(me_owner, partner(me_group, step, groups)), device_id_type=MESH
        )


def enter(me_owner, me_group, owners, groups):
    greet(me_owner, me_group, owners, groups)
    pl.semaphore_wait(pltpu.get_barrier_semaphore(), owners + groups - 2)


def spread_kernel(owners, groups, pieces, *refs):
    sources, dests = refs[0:2], refs[2:4]
    a_send, a_recv, b_send, b_recv, c_send, c_recv = refs[4:]
    me_owner, me_group = lax.axis_index("owner"), lax.axis_index("dp")
    per_piece = owners // pieces
    relay = groups == 4
    direct = [1, 2] if relay else list(range(1, groups))
    enter(me_owner, me_group, owners, groups)
    sends = []

    for step in range(1, owners):
        peer = partner(me_owner, step, owners)
        for which in range(2):
            copy = pltpu.make_async_remote_copy(
                src_ref=sources[which].at[peer],
                dst_ref=dests[which].at[me_group, me_owner],
                send_sem=a_send.at[which, step],
                recv_sem=a_recv.at[which, step],
                device_id=(peer, me_group),
                device_id_type=MESH,
            )
            copy.start()
            sends.append(copy)
    for which in range(2):
        dests[which][me_group, me_owner] = sources[which][me_owner]

    def piece_of(group, piece):
        here = partner(me_owner // per_piece, piece, pieces) * per_piece
        return group, pl.ds(here, per_piece)

    def hop(which, group, piece, step, send_sem, recv_sem):
        group_at, rows_at = piece_of(group, piece)
        return pltpu.make_async_remote_copy(
            src_ref=dests[which].at[group_at, rows_at],
            dst_ref=dests[which].at[group_at, rows_at],
            send_sem=send_sem,
            recv_sem=recv_sem,
            device_id=(me_owner, partner(me_group, step, groups)),
            device_id_type=MESH,
        )

    def forward(piece):
        for which in range(2):
            near, far = (1, 2) if which == 0 else (2, 1)
            group = partner(me_group, near, groups)
            hop(which, group, piece, near, b_send.at[which, near, piece], b_recv.at[which, near, piece]).wait_recv()
            copy = hop(which, group, piece, far, c_send.at[which, piece], c_recv.at[which, piece])
            copy.start()
            sends.append(copy)

    for piece in range(pieces):
        for inner in range(per_piece):
            step = piece * per_piece + inner
            if step == 0:
                continue
            peer = partner(me_owner, step, owners)
            for which in range(2):
                pltpu.make_async_remote_copy(
                    src_ref=sources[which].at[peer],
                    dst_ref=dests[which].at[me_group, peer],
                    send_sem=a_send.at[which, step],
                    recv_sem=a_recv.at[which, step],
                    device_id=(peer, me_group),
                    device_id_type=MESH,
                ).wait_recv()
        for step in direct:
            for which in range(2):
                copy = hop(which, me_group, piece, step, b_send.at[which, step, piece], b_recv.at[which, step, piece])
                copy.start()
                sends.append(copy)
        if relay and piece >= 1:
            forward(piece - 1)
    if relay:
        forward(pieces - 1)
    for piece in range(pieces):
        for which in range(2):
            for step in direct:
                if relay and step == (1 if which == 0 else 2):
                    continue
                group = partner(me_group, step, groups)
                hop(which, group, piece, step, b_send.at[which, step, piece], b_recv.at[which, step, piece]).wait_recv()
            if relay:
                group = partner(me_group, 3, groups)
                hop(which, group, piece, 1 if which else 2, c_send.at[which, piece], c_recv.at[which, piece]).wait_recv()
    for copy in sends:
        copy.wait_send()


def collect_kernel(owners, groups, pieces, parts, back, landed, summed, b_send, b_recv, a_send, a_recv):
    me_owner, me_group = lax.axis_index("owner"), lax.axis_index("dp")
    per_piece = owners // pieces
    enter(me_owner, me_group, owners, groups)
    sends = []

    def share(piece, step):
        here = pl.ds(partner(me_owner // per_piece, piece, pieces) * per_piece, per_piece)
        peer = partner(me_group, step, groups)
        return pltpu.make_async_remote_copy(
            src_ref=parts.at[peer, here],
            dst_ref=landed.at[step - 1, here],
            send_sem=b_send.at[step, piece],
            recv_sem=b_recv.at[step, piece],
            device_id=(me_owner, peer),
            device_id_type=MESH,
        )

    order = list(range(pieces))[::-1]
    for piece in order:
        for step in list(range(1, groups))[::-1]:
            copy = share(piece, step)
            copy.start()
            sends.append(copy)

    def ship(step):
        peer = partner(me_owner, step, owners)
        return pltpu.make_async_remote_copy(
            src_ref=summed.at[peer],
            dst_ref=back.at[me_owner],
            send_sem=a_send.at[step],
            recv_sem=a_recv.at[step],
            device_id=(peer, me_group),
            device_id_type=MESH,
        )

    for piece in order:
        for step in range(1, groups):
            share(piece, step).wait_recv()
        for inner in range(per_piece):
            step = piece * per_piece + inner
            peer = partner(me_owner, step, owners)
            total = parts[me_group, peer].astype(jnp.float32)
            for other in range(1, groups):
                total = total + landed[other - 1, peer].astype(jnp.float32)
            rounded = total.astype(jnp.bfloat16)
            if step == 0:
                back[peer] = rounded
            else:
                summed[peer] = rounded
                copy = ship(step)
                copy.start()
                sends.append(copy)
    for step in range(1, owners):
        peer = partner(me_owner, step, owners)
        pltpu.make_async_remote_copy(
            src_ref=summed.at[peer],
            dst_ref=back.at[peer],
            send_sem=a_send.at[step],
            recv_sem=a_recv.at[step],
            device_id=(peer, me_group),
            device_id_type=MESH,
        ).wait_recv()
    for copy in sends:
        copy.wait_send()


def spread(send_inputs, send_upstream, owners, groups):
    _, slots, width = send_inputs.shape
    pieces = owners // 2 if groups == 4 else 1
    whole = jax.ShapeDtypeStruct((groups, owners, slots, width), jnp.bfloat16)
    vmem = pl.BlockSpec(memory_space=pltpu.VMEM)
    dma = pltpu.SemaphoreType.DMA
    return pl.pallas_call(
        functools.partial(spread_kernel, owners, groups, pieces),
        out_shape=(whole, whole),
        in_specs=[vmem, vmem],
        out_specs=(vmem, vmem),
        scratch_shapes=[
            dma((2, owners)),
            dma((2, owners)),
            dma((2, groups, pieces)),
            dma((2, groups, pieces)),
            dma((2, pieces)),
            dma((2, pieces)),
        ],
        compiler_params=pltpu.CompilerParams(
            collective_id=0, has_side_effects=True, vmem_limit_bytes=24 << 20
        ),
    )(send_inputs, send_upstream)


def collect(parts, owners, groups):
    _, _, slots, width = parts.shape
    pieces = owners // 2 if groups == 4 else 1
    vmem = pl.BlockSpec(memory_space=pltpu.VMEM)
    dma = pltpu.SemaphoreType.DMA
    return pl.pallas_call(
        functools.partial(collect_kernel, owners, groups, pieces),
        out_shape=jax.ShapeDtypeStruct((owners, slots, width), jnp.bfloat16),
        in_specs=[vmem],
        out_specs=vmem,
        scratch_shapes=[
            pltpu.VMEM((groups - 1, owners, slots, width), jnp.bfloat16),
            pltpu.VMEM((owners, slots, width), jnp.bfloat16),
            dma((groups, pieces)),
            dma((groups, pieces)),
            dma((owners,)),
            dma((owners,)),
        ],
        compiler_params=pltpu.CompilerParams(
            collective_id=1, has_side_effects=True, vmem_limit_bytes=24 << 20
        ),
    )(parts)


def fused_kernel(owners, pieces, scale, *refs):
    (ids, arrivals, up_hbm, down_hbm), refs = refs[0:4], refs[4:]
    tok_count = ids.shape[1]
    (input_grad, grad_up, grad_down), refs = refs[0:3], refs[3:]
    (hidden, pre_grad), refs = refs[0:2], refs[2:]
    back, refs = refs[0], refs[1:]
    sources, dests, up, down, parts, landed, summed = refs[0:7]
    w_sem, a_send, a_recv, b_recv, c_recv, d_sends, e_recv = refs[7:]
    groups = 4
    slots, width = sources.shape[2:]
    units = up.shape[1]
    step_rows = groups * slots
    relayed = tuple(range(8))
    summed_twice = pieces[0:0]
    unit_tile, wide = units // 2, width // 2
    me_owner, me_group = lax.axis_index("owner"), lax.axis_index("dp")
    greet(me_owner, me_group, owners, groups)
    weight_copies = [
        pltpu.make_async_copy(up_hbm, up, w_sem.at[0]),
        pltpu.make_async_copy(down_hbm, down, w_sem.at[1]),
    ]
    for copy in weight_copies:
        copy.start()
    row_ids = ids[...]
    square = (tok_count, tok_count)
    first_at = lax.broadcasted_iota(jnp.int32, square, 0)
    second_at = lax.broadcasted_iota(jnp.int32, square, 1)
    spread_ids = jnp.broadcast_to(row_ids.astype(jnp.float32), square)
    column_ids = jnp.sum(jnp.where(first_at == second_at, spread_ids, 0.0), axis=1, keepdims=True)
    same = jnp.logical_and(column_ids == spread_ids, first_at < second_at)
    ranks = jnp.sum(jnp.where(same, 1.0, 0.0), axis=0, keepdims=True).astype(jnp.int32)
    target = jnp.bitwise_xor(row_ids, me_owner) * slots + ranks
    positions = lax.broadcasted_iota(jnp.int32, (owners * slots, tok_count), 0)
    placer = jnp.where(positions == target, 1.0, 0.0).astype(jnp.bfloat16)
    for which in range(2):
        placed = jnp.dot(placer, arrivals[which * tok_count : (which + 1) * tok_count, :], preferred_element_type=jnp.float32)
        for step in range(owners):
            block = placed[step * slots : (step + 1) * slots, :].astype(jnp.bfloat16)
            (sources if step else dests)[(which, step) if step else (which, 0, 0)] = block
    pl.semaphore_wait(pltpu.get_barrier_semaphore(), owners + groups - 2)

    def along_owner(source, dest, step, send_sem, recv_sem):
        return pltpu.make_async_remote_copy(
            src_ref=source,
            dst_ref=dest,
            send_sem=send_sem,
            recv_sem=recv_sem,
            device_id=(partner(me_owner, step, owners), me_group),
            device_id_type=MESH,
        )

    def along_group(source, dest, step, send_sem, recv_sem):
        return pltpu.make_async_remote_copy(
            src_ref=source,
            dst_ref=dest,
            send_sem=send_sem,
            recv_sem=recv_sem,
            device_id=(me_owner, partner(me_group, step, groups)),
            device_id_type=MESH,
        )

    def out_copy(step):
        return along_owner(sources.at[:, step], dests.at[:, step, 0], step, a_send, a_recv.at[step - 1])

    def near_copy(step, side):
        return along_group(
            dests.at[:, step, 0], dests.at[:, step, side], side, d_sends.at[0 if side < 3 else 1], b_recv.at[side - 1, step]
        )

    def relay_copy(which, step):
        first, second = (1, 2) if which == 0 else (2, 1)
        return along_group(
            dests.at[which, step, first], dests.at[which, step, 3], second, d_sends.at[2], b_recv.at[2, step]
        )

    def part_slice(piece, chunk):
        return pl.ds(piece[0], len(piece)), pl.ds(chunk * wide, wide)

    def part_copy(piece, chunk, side, slot, towards, leg):
        here, cols = part_slice(piece, chunk)
        return along_group(
            parts.at[here, side, :, cols],
            landed.at[here, slot, :, cols],
            towards,
            d_sends.at[3],
            c_recv.at[leg, pieces.index(piece), chunk],
        )

    def parts_landed(piece, chunk, slots_in, leg):
        here, cols = part_slice(piece, chunk)
        whole = landed.at[here, slots_in, :, cols]
        along_group(whole, whole, 1, d_sends.at[3], c_recv.at[leg, pieces.index(piece), chunk]).wait_recv()

    def back_copy(step, chunk):
        cols = pl.ds(chunk * wide, wide)
        return along_owner(summed.at[step, :, cols], back.at[step, :, cols], step, d_sends.at[4], e_recv.at[chunk])

    def out(*steps):
        for step in steps:
            out_copy(step).start()

    def arrive(*steps):
        for step in steps:
            if step:
                out_copy(step).wait_recv()
            for side in (1, 2) if step in relayed else (3, 1, 2):
                near_copy(step, side).start()

    def forward(*steps):
        for step in steps:
            for side in (1, 2):
                near_copy(step, side).wait_recv()
            for which in range(2):
                relay_copy(which, step).start()

    def gather(piece):
        for step in piece:
            for side in (3,) if step in relayed else (1, 2, 3):
                near_copy(step, side).wait_recv()

    def activate(piece, tile):
        here = pl.ds(piece[0] * step_rows, len(piece) * step_rows)
        steps = pl.ds(piece[0], len(piece))
        cols = pl.ds(tile * unit_tile, unit_tile)
        row_count = len(piece) * step_rows
        pre_act = jnp.dot(dests[0, steps].reshape(row_count, width), up[:, cols], preferred_element_type=jnp.float32)
        hidden_grad = lax.dot_general(
            dests[1, steps].reshape(row_count, width), down[cols, :], (((1,), (1,)), ((), ())), preferred_element_type=jnp.float32
        )
        activated, pullback = jax.vjp(jax.nn.gelu, pre_act)
        hidden[here, cols] = activated.astype(jnp.bfloat16)
        pre_grad[here, cols] = pullback(hidden_grad)[0].astype(jnp.bfloat16)

    def project(piece, chunk):
        here = pl.ds(piece[0] * step_rows, len(piece) * step_rows)
        cols = pl.ds(chunk * wide, wide)
        part = lax.dot_general(
            pre_grad[here, :], up[cols, :], (((1,), (1,)), ((), ())), preferred_element_type=jnp.float32
        )
        for at in range(len(piece) * groups):
            step, group = piece[at // groups], at % groups
            parts[step, group, :, cols] = part[at * slots : (at + 1) * slots, :].astype(jnp.bfloat16)
        if piece in summed_twice:
            near = 1 + chunk
            part_copy(piece, chunk, 3, 1, near, 0).start()
            part_copy(piece, chunk, near, 0, near, 0).start()
        else:
            for side in (3, 1, 2):
                part_copy(piece, chunk, side, side - 1, side, 0).start()

    def relay_sum(piece, chunk):
        parts_landed(piece, chunk, pl.ds(0, 2), 0)
        here, cols = part_slice(piece, chunk)
        far = 2 - chunk
        total = parts[here, far, :, cols].astype(jnp.float32) + landed[here, 1, :, cols].astype(jnp.float32)
        parts[here, far, :, cols] = total.astype(jnp.bfloat16)
        part_copy(piece, chunk, far, 2, far, 1).start()

    def reduce(piece, chunk):
        cols = pl.ds(chunk * wide, wide)
        others = (0, 2) if piece in summed_twice else (0, 1, 2)
        if piece in summed_twice:
            parts_landed(piece, chunk, pl.ds(2, 1), 1)
        else:
            parts_landed(piece, chunk, pl.ds(0, 3), 0)
        for step in piece[::-1]:
            total = parts[step, 0, :, cols].astype(jnp.float32)
            for other in others:
                total = total + landed[step, other, :, cols].astype(jnp.float32)
            rounded = total.astype(jnp.bfloat16)
            if step == 0:
                back[0, :, cols] = rounded
            else:
                summed[step, :, cols] = rounded
                back_copy(step, chunk).start()

    def weight_grad(which, other, out):
        tile = 512
        row_count = owners * step_rows

        def one(index, carry):
            cols = pl.ds(pl.multiple_of(index * tile, tile), tile)
            if which == 0:
                left, right = dests[0, :, :, :, cols].reshape(row_count, tile), other[...]
            else:
                left, right = other[:, cols], dests[1].reshape(row_count, width)
            term = lax.dot_general(left, right, (((0,), (0,)), ((), ())), preferred_element_type=jnp.float32)
            out[cols, :] = (term * scale).astype(jnp.bfloat16)
            return carry

        lax.fori_loop(0, out.shape[0] // tile, one, 0)

    out(1)
    out(4)
    out(5)
    arrive(0)
    out(2)
    out(3)
    arrive(1)
    forward(0)
    forward(1)
    arrive(2)
    arrive(3)
    out(6)
    out(7)
    for copy in weight_copies:
        copy.wait()
    gather(pieces[0])
    activate(pieces[0], 0)
    arrive(4)
    arrive(5)
    forward(2)
    forward(3)
    activate(pieces[0], 1)
    arrive(6)
    arrive(7)
    forward(4)
    forward(5)
    project(pieces[0], 0)
    project(pieces[0], 1)
    gather(pieces[1])
    activate(pieces[1], 0)
    forward(6)
    forward(7)
    activate(pieces[1], 1)
    project(pieces[1], 0)
    project(pieces[1], 1)
    gather(pieces[2])
    activate(pieces[2], 0)
    reduce(pieces[0], 0)
    reduce(pieces[0], 1)
    activate(pieces[2], 1)
    project(pieces[2], 0)
    project(pieces[2], 1)
    reduce(pieces[1], 0)
    reduce(pieces[1], 1)
    weight_grad(0, pre_grad, grad_up)
    reduce(pieces[2], 0)
    reduce(pieces[2], 1)
    weight_grad(1, hidden, grad_down)
    for chunk in range(2):
        whole = back.at[1:owners, :, pl.ds(chunk * wide, wide)]
        along_owner(whole, whole, 1, d_sends.at[4], e_recv.at[chunk]).wait_recv()
    returned = jnp.concatenate([back[step].astype(jnp.float32) for step in range(owners)], axis=0)
    adapter_grad = lax.dot_general(
        placer, returned.astype(jnp.bfloat16), (((0,), (0,)), ((), ())), preferred_element_type=jnp.float32
    )
    input_grad[...] = (arrivals[tok_count : 2 * tok_count, :].astype(jnp.float32) + adapter_grad).astype(jnp.bfloat16)
    sent = [(sources.at[:, 1:owners], a_send), (dests.at[:, :, 1:3], d_sends.at[0])]
    if len(relayed) < owners:
        sent.append((dests.at[:, len(relayed) : owners, 3], d_sends.at[1]))
    sent += [(dests.at[:, 0 : len(relayed), 3], d_sends.at[2]), (landed, d_sends.at[3])]
    sent.append((back.at[1:owners], d_sends.at[4]))
    for whole, sem in sent:
        along_owner(whole, whole, 1, sem, sem).wait_send()


def fused(lang_ids, tokens, upstream, up_matrix, down_matrix, scale, owners, slots):
    width = tokens.shape[1]
    units = up_matrix.shape[1]
    groups = 4
    pieces = ((0, 1), (2, 3, 4, 5), (6, 7))
    total = owners * groups * slots
    vmem = pl.BlockSpec(memory_space=pltpu.VMEM)
    anywhere = pl.BlockSpec(memory_space=pltpu.HBM)
    dma = pltpu.SemaphoreType.DMA
    bf16 = jnp.bfloat16
    grid = (owners, groups, slots, width)
    held = [((total, units), bf16), ((total, units), bf16)]
    outs = [(tokens.shape, bf16), ((width, units), bf16), ((units, width), bf16)]
    return pl.pallas_call(
        functools.partial(fused_kernel, owners, pieces, scale),
        out_shape=[jax.ShapeDtypeStruct(*item) for item in outs],
        in_specs=[vmem] * 2 + [anywhere] * 2,
        out_specs=[vmem] * len(outs),
        scratch_shapes=[pltpu.VMEM(*item) for item in held]
        + [
            pltpu.VMEM((owners, slots, width), bf16),
            pltpu.VMEM((2, owners, slots, width), bf16),
            pltpu.VMEM((2,) + grid, bf16),
            pltpu.VMEM((width, units), bf16),
            pltpu.VMEM((units, width), bf16),
            pltpu.VMEM(grid, bf16),
            pltpu.VMEM((owners, groups - 1, slots, width), bf16),
            pltpu.VMEM((owners, slots, width), bf16),
            dma((2,)),
            dma,
            dma((owners - 1,)),
            dma((3, owners)),
            dma((2, len(pieces), 2)),
            dma((5,)),
            dma((2,)),
        ],
        compiler_params=pltpu.CompilerParams(
            collective_id=2, has_side_effects=True, vmem_limit_bytes=44 << 20
        ),
    )(lang_ids[None], jnp.concatenate([tokens, upstream], axis=0), up_matrix, down_matrix)


def publish_kernel(count, splits, *refs):
    sources, dests, sem = refs[:count], refs[count : 2 * count], refs[2 * count]
    copies = []
    for at, (source, dest) in enumerate(zip(sources, dests)):
        rows = source.shape[0] // splits[at]
        for part in range(splits[at]):
            here = pl.ds(part * rows, rows)
            copies.append(
                pltpu.make_async_copy(source.at[here], dest.at[here], sem.at[sum(splits[:at]) + part])
            )
    for copy in copies:
        copy.start()
    for copy in copies:
        copy.wait()


def publish(*arrays):
    splits = [4 if array.shape[0] % 64 == 0 else 1 for array in arrays]
    anywhere = pl.BlockSpec(memory_space=pl.ANY)
    return pl.pallas_call(
        functools.partial(publish_kernel, len(arrays), splits),
        out_shape=[jax.ShapeDtypeStruct(array.shape, array.dtype) for array in arrays],
        in_specs=[pl.BlockSpec(memory_space=pltpu.VMEM)] * len(arrays),
        out_specs=[anywhere] * len(arrays),
        scratch_shapes=[pltpu.SemaphoreType.DMA((sum(splits),))],
        compiler_params=pltpu.CompilerParams(vmem_limit_bytes=16 << 20),
    )(*arrays)


def placement_matrix(block_ids, owners, slot_count):
    tok_count = block_ids.shape[0]
    matches = block_ids[:, None] == block_ids[None, :]
    positions = jnp.arange(tok_count, dtype=jnp.int32)
    earlier = positions[None, :] < positions[:, None]
    slots = jnp.sum(jnp.logical_and(matches, earlier), axis=1)
    target = block_ids * slot_count + slots
    return (target[None, :] == jnp.arange(owners * slot_count, dtype=jnp.int32)[:, None]).astype(
        jnp.bfloat16
    )


def local(tokens, upstream, lang_ids, up_weight, down_weight):
    owners = lax.axis_size("owner")
    groups = lax.axis_size("dp")
    tok_count, width = tokens.shape
    slots = max(2, 4 * tok_count // (3 * owners))
    rows_here = owners * slots
    up_matrix = up_weight[0]
    down_matrix = down_weight[0]
    grad_scale = float(tok_count * groups) ** (-0.5)
    one_kernel = (
        groups == 4
        and slots == 8
        and owners == 8
        and width % 512 == 0
        and up_matrix.shape[1] % 512 == 0
    )
    if one_kernel:
        input_grad, grad_up, grad_down = fused(
            lang_ids, tokens, upstream, up_matrix, down_matrix, grad_scale, owners, slots
        )
        input_grad, grad_up, grad_down = publish(input_grad, grad_up, grad_down)
        return (input_grad, grad_up[None], grad_down[None])
    placer = placement_matrix(lang_ids, owners, slots)
    send_inputs = jnp.dot(placer, tokens, preferred_element_type=jnp.float32).astype(jnp.bfloat16)
    send_upstream = jnp.dot(placer, upstream, preferred_element_type=jnp.float32).astype(jnp.bfloat16)
    send_inputs = send_inputs.reshape(owners, slots, width)
    send_upstream = send_upstream.reshape(owners, slots, width)
    row_inputs, row_upstream = spread(
        send_inputs,
        send_upstream,
        owners,
        groups,
    )
    row_inputs = row_inputs.reshape(groups * rows_here, width)
    row_upstream = row_upstream.reshape(groups * rows_here, width)
    pre_act = jnp.dot(row_inputs, up_matrix, preferred_element_type=jnp.float32)
    activated, pullback = jax.vjp(jax.nn.gelu, pre_act)
    hidden = activated.astype(jnp.bfloat16)
    hidden_grad = lax.dot_general(
        row_upstream, down_matrix, (((1,), (1,)), ((), ())), preferred_element_type=jnp.float32
    )
    pre_grad = pullback(hidden_grad)[0].astype(jnp.bfloat16)
    parts = lax.dot_general(
        pre_grad, up_matrix, (((1,), (1,)), ((), ())), preferred_element_type=jnp.float32
    ).astype(jnp.bfloat16)
    returned = collect(parts.reshape(groups, owners, slots, width), owners, groups)
    up_term = lax.dot_general(
        row_inputs, pre_grad, (((0,), (0,)), ((), ())), preferred_element_type=jnp.float32
    )
    down_term = lax.dot_general(
        hidden, row_upstream, (((0,), (0,)), ((), ())), preferred_element_type=jnp.float32
    )
    grad_up = (up_term * grad_scale).astype(jnp.bfloat16)
    grad_down = (down_term * grad_scale).astype(jnp.bfloat16)
    adapter_grad = lax.dot_general(
        placer,
        returned.reshape(rows_here, width),
        (((0,), (0,)), ((), ())),
        preferred_element_type=jnp.float32,
    )
    input_grad = (upstream.astype(jnp.float32) + adapter_grad).astype(jnp.bfloat16)
    return (input_grad, grad_up[None], grad_down[None])


def solution(mesh):
    in_specs = (
        P(("owner", "dp"), None),
        P(("owner", "dp"), None),
        P(("owner", "dp")),
        P("owner", None, "dp"),
        P("owner", "dp", None),
    )
    out_specs = (P(("owner", "dp"), None), P("owner", None, "dp"), P("owner", "dp", None))
    return jax.shard_map(local, mesh=mesh, in_specs=in_specs, out_specs=out_specs, check_vma=False)
```

```python
import functools

import jax
import jax.numpy as jnp
from jax import lax
from jax.experimental import pallas as pl
from jax.experimental.pallas import tpu as pltpu
from jax.sharding import PartitionSpec as P

MESH = pl.DeviceIdType.MESH


def partner(index, step, count):
    total, bit = 0, 1
    while bit < count:
        digit = (index // bit) % 2
        total = total + bit * ((1 - digit) if (step // bit) % 2 else digit)
        bit *= 2
    return total


def greet(me_owner, me_group, owners, groups):
    barrier = pltpu.get_barrier_semaphore()
    for step in range(1, owners):
        pl.semaphore_signal(
            barrier, inc=1, device_id=(partner(me_owner, step, owners), me_group), device_id_type=MESH
        )
    for step in range(1, groups):
        pl.semaphore_signal(
            barrier, inc=1, device_id=(me_owner, partner(me_group, step, groups)), device_id_type=MESH
        )


def enter(me_owner, me_group, owners, groups):
    greet(me_owner, me_group, owners, groups)
    pl.semaphore_wait(pltpu.get_barrier_semaphore(), owners + groups - 2)


def spread_kernel(owners, groups, pieces, *refs):
    sources, dests = refs[0:2], refs[2:4]
    a_send, a_recv, b_send, b_recv, c_send, c_recv = refs[4:]
    me_owner, me_group = lax.axis_index("owner"), lax.axis_index("dp")
    per_piece = owners // pieces
    relay = groups == 4
    direct = [1, 2] if relay else list(range(1, groups))
    enter(me_owner, me_group, owners, groups)
    sends = []

    for step in range(1, owners):
        peer = partner(me_owner, step, owners)
        for which in range(2):
            copy = pltpu.make_async_remote_copy(
                src_ref=sources[which].at[peer],
                dst_ref=dests[which].at[me_group, me_owner],
                send_sem=a_send.at[which, step],
                recv_sem=a_recv.at[which, step],
                device_id=(peer, me_group),
                device_id_type=MESH,
            )
            copy.start()
            sends.append(copy)
    for which in range(2):
        dests[which][me_group, me_owner] = sources[which][me_owner]

    def piece_of(group, piece):
        here = partner(me_owner // per_piece, piece, pieces) * per_piece
        return group, pl.ds(here, per_piece)

    def hop(which, group, piece, step, send_sem, recv_sem):
        group_at, rows_at = piece_of(group, piece)
        return pltpu.make_async_remote_copy(
            src_ref=dests[which].at[group_at, rows_at],
            dst_ref=dests[which].at[group_at, rows_at],
            send_sem=send_sem,
            recv_sem=recv_sem,
            device_id=(me_owner, partner(me_group, step, groups)),
            device_id_type=MESH,
        )

    def forward(piece):
        for which in range(2):
            near, far = (1, 2) if which == 0 else (2, 1)
            group = partner(me_group, near, groups)
            hop(which, group, piece, near, b_send.at[which, near, piece], b_recv.at[which, near, piece]).wait_recv()
            copy = hop(which, group, piece, far, c_send.at[which, piece], c_recv.at[which, piece])
            copy.start()
            sends.append(copy)

    for piece in range(pieces):
        for inner in range(per_piece):
            step = piece * per_piece + inner
            if step == 0:
                continue
            peer = partner(me_owner, step, owners)
            for which in range(2):
                pltpu.make_async_remote_copy(
                    src_ref=sources[which].at[peer],
                    dst_ref=dests[which].at[me_group, peer],
                    send_sem=a_send.at[which, step],
                    recv_sem=a_recv.at[which, step],
                    device_id=(peer, me_group),
                    device_id_type=MESH,
                ).wait_recv()
        for step in direct:
            for which in range(2):
                copy = hop(which, me_group, piece, step, b_send.at[which, step, piece], b_recv.at[which, step, piece])
                copy.start()
                sends.append(copy)
        if relay and piece >= 1:
            forward(piece - 1)
    if relay:
        forward(pieces - 1)
    for piece in range(pieces):
        for which in range(2):
            for step in direct:
                if relay and step == (1 if which == 0 else 2):
                    continue
                group = partner(me_group, step, groups)
                hop(which, group, piece, step, b_send.at[which, step, piece], b_recv.at[which, step, piece]).wait_recv()
            if relay:
                group = partner(me_group, 3, groups)
                hop(which, group, piece, 1 if which else 2, c_send.at[which, piece], c_recv.at[which, piece]).wait_recv()
    for copy in sends:
        copy.wait_send()


def collect_kernel(owners, groups, pieces, parts, back, landed, summed, b_send, b_recv, a_send, a_recv):
    me_owner, me_group = lax.axis_index("owner"), lax.axis_index("dp")
    per_piece = owners // pieces
    enter(me_owner, me_group, owners, groups)
    sends = []

    def share(piece, step):
        here = pl.ds(partner(me_owner // per_piece, piece, pieces) * per_piece, per_piece)
        peer = partner(me_group, step, groups)
        return pltpu.make_async_remote_copy(
            src_ref=parts.at[peer, here],
            dst_ref=landed.at[step - 1, here],
            send_sem=b_send.at[step, piece],
            recv_sem=b_recv.at[step, piece],
            device_id=(me_owner, peer),
            device_id_type=MESH,
        )

    order = list(range(pieces))[::-1]
    for piece in order:
        for step in list(range(1, groups))[::-1]:
            copy = share(piece, step)
            copy.start()
            sends.append(copy)

    def ship(step):
        peer = partner(me_owner, step, owners)
        return pltpu.make_async_remote_copy(
            src_ref=summed.at[peer],
            dst_ref=back.at[me_owner],
            send_sem=a_send.at[step],
            recv_sem=a_recv.at[step],
            device_id=(peer, me_group),
            device_id_type=MESH,
        )

    for piece in order:
        for step in range(1, groups):
            share(piece, step).wait_recv()
        for inner in range(per_piece):
            step = piece * per_piece + inner
            peer = partner(me_owner, step, owners)
            total = parts[me_group, peer].astype(jnp.float32)
            for other in range(1, groups):
                total = total + landed[other - 1, peer].astype(jnp.float32)
            rounded = total.astype(jnp.bfloat16)
            if step == 0:
                back[peer] = rounded
            else:
                summed[peer] = rounded
                copy = ship(step)
                copy.start()
                sends.append(copy)
    for step in range(1, owners):
        peer = partner(me_owner, step, owners)
        pltpu.make_async_remote_copy(
            src_ref=summed.at[peer],
            dst_ref=back.at[peer],
            send_sem=a_send.at[step],
            recv_sem=a_recv.at[step],
            device_id=(peer, me_group),
            device_id_type=MESH,
        ).wait_recv()
    for copy in sends:
        copy.wait_send()


def spread(send_inputs, send_upstream, owners, groups):
    _, slots, width = send_inputs.shape
    pieces = owners // 2 if groups == 4 else 1
    whole = jax.ShapeDtypeStruct((groups, owners, slots, width), jnp.bfloat16)
    vmem = pl.BlockSpec(memory_space=pltpu.VMEM)
    dma = pltpu.SemaphoreType.DMA
    return pl.pallas_call(
        functools.partial(spread_kernel, owners, groups, pieces),
        out_shape=(whole, whole),
        in_specs=[vmem, vmem],
        out_specs=(vmem, vmem),
        scratch_shapes=[
            dma((2, owners)),
            dma((2, owners)),
            dma((2, groups, pieces)),
            dma((2, groups, pieces)),
            dma((2, pieces)),
            dma((2, pieces)),
        ],
        compiler_params=pltpu.CompilerParams(
            collective_id=0, has_side_effects=True, vmem_limit_bytes=24 << 20
        ),
    )(send_inputs, send_upstream)


def collect(parts, owners, groups):
    _, _, slots, width = parts.shape
    pieces = owners // 2 if groups == 4 else 1
    vmem = pl.BlockSpec(memory_space=pltpu.VMEM)
    dma = pltpu.SemaphoreType.DMA
    return pl.pallas_call(
        functools.partial(collect_kernel, owners, groups, pieces),
        out_shape=jax.ShapeDtypeStruct((owners, slots, width), jnp.bfloat16),
        in_specs=[vmem],
        out_specs=vmem,
        scratch_shapes=[
            pltpu.VMEM((groups - 1, owners, slots, width), jnp.bfloat16),
            pltpu.VMEM((owners, slots, width), jnp.bfloat16),
            dma((groups, pieces)),
            dma((groups, pieces)),
            dma((owners,)),
            dma((owners,)),
        ],
        compiler_params=pltpu.CompilerParams(
            collective_id=1, has_side_effects=True, vmem_limit_bytes=24 << 20
        ),
    )(parts)


def fused_kernel(owners, pieces, chunk_counts, scale, *refs):
    (ids, arrivals, up_hbm, down_hbm), refs = refs[0:4], refs[4:]
    tok_count = ids.shape[1]
    (back, placer_out, kept, grad_up, grad_down), refs = refs[0:5], refs[5:]
    (hidden, pre_grad), refs = refs[0:2], refs[2:]
    sources, dests, up, down, parts, landed, summed = refs[0:7]
    w_sem, a_send, a_recv, b_recv, c_recv, d_sends, e_recv = refs[7:]
    groups = 4
    slots, width = sources.shape[2:]
    units = up.shape[1]
    step_rows = groups * slots
    relayed = tuple(range(8))
    summed_twice = pieces[0:0]
    unit_tile = units // 2
    me_owner, me_group = lax.axis_index("owner"), lax.axis_index("dp")
    greet(me_owner, me_group, owners, groups)
    weight_copies = [
        pltpu.make_async_copy(up_hbm, up, w_sem.at[0]),
        pltpu.make_async_copy(down_hbm, down, w_sem.at[1]),
    ]
    for copy in weight_copies:
        copy.start()
    row_ids = ids[...]
    square = (tok_count, tok_count)
    first_at = lax.broadcasted_iota(jnp.int32, square, 0)
    second_at = lax.broadcasted_iota(jnp.int32, square, 1)
    spread_ids = jnp.broadcast_to(row_ids.astype(jnp.float32), square)
    column_ids = jnp.sum(jnp.where(first_at == second_at, spread_ids, 0.0), axis=1, keepdims=True)
    same = jnp.logical_and(column_ids == spread_ids, first_at < second_at)
    ranks = jnp.sum(jnp.where(same, 1.0, 0.0), axis=0, keepdims=True).astype(jnp.int32)
    target = jnp.bitwise_xor(row_ids, me_owner) * slots + ranks
    positions = lax.broadcasted_iota(jnp.int32, (owners * slots, tok_count), 0)
    placer = jnp.where(positions == target, 1.0, 0.0).astype(jnp.bfloat16)
    placer_out[...] = placer
    kept[...] = arrivals[tok_count : 2 * tok_count, :]
    for which in range(2):
        placed = jnp.dot(placer, arrivals[which * tok_count : (which + 1) * tok_count, :], preferred_element_type=jnp.float32)
        for step in range(owners):
            block = placed[step * slots : (step + 1) * slots, :].astype(jnp.bfloat16)
            (sources if step else dests)[(which, step) if step else (which, 0, 0)] = block
    pl.semaphore_wait(pltpu.get_barrier_semaphore(), owners + groups - 2)

    def along_owner(source, dest, step, send_sem, recv_sem):
        return pltpu.make_async_remote_copy(
            src_ref=source,
            dst_ref=dest,
            send_sem=send_sem,
            recv_sem=recv_sem,
            device_id=(partner(me_owner, step, owners), me_group),
            device_id_type=MESH,
        )

    def along_group(source, dest, step, send_sem, recv_sem):
        return pltpu.make_async_remote_copy(
            src_ref=source,
            dst_ref=dest,
            send_sem=send_sem,
            recv_sem=recv_sem,
            device_id=(me_owner, partner(me_group, step, groups)),
            device_id_type=MESH,
        )

    def out_copy(step):
        return along_owner(sources.at[:, step], dests.at[:, step, 0], step, a_send, a_recv.at[step - 1])

    def near_copy(step, side):
        return along_group(
            dests.at[:, step, 0], dests.at[:, step, side], side, d_sends.at[0 if side < 3 else 1], b_recv.at[side - 1, step]
        )

    def relay_copy(which, step):
        first, second = (1, 2) if which == 0 else (2, 1)
        return along_group(
            dests.at[which, step, first], dests.at[which, step, 3], second, d_sends.at[2], b_recv.at[2, step]
        )

    def columns(piece, chunk):
        size = width // chunk_counts[pieces.index(piece)]
        return pl.ds(chunk * size, size)

    def part_slice(piece, chunk):
        return pl.ds(piece[0], len(piece)), columns(piece, chunk)

    def part_copy(piece, chunk, side, slot, towards, leg):
        here, cols = part_slice(piece, chunk)
        return along_group(
            parts.at[here, side, :, cols],
            landed.at[here, slot, :, cols],
            towards,
            d_sends.at[3],
            c_recv.at[leg, pieces.index(piece), chunk],
        )

    def parts_landed(piece, chunk, slots_in, leg):
        here, cols = part_slice(piece, chunk)
        whole = landed.at[here, slots_in, :, cols]
        along_group(whole, whole, 1, d_sends.at[3], c_recv.at[leg, pieces.index(piece), chunk]).wait_recv()

    def back_copy(step, cols):
        return along_owner(summed.at[step, :, cols], back.at[step, :, cols], step, d_sends.at[4], e_recv)

    def out(*steps):
        for step in steps:
            out_copy(step).start()

    def arrive(*steps):
        for step in steps:
            if step:
                out_copy(step).wait_recv()
            for side in (1, 2) if step in relayed else (3, 1, 2):
                near_copy(step, side).start()

    def forward(*steps):
        for step in steps:
            for side in (1, 2):
                near_copy(step, side).wait_recv()
            for which in range(2):
                relay_copy(which, step).start()

    def gather(piece):
        for step in piece:
            for side in (3,) if step in relayed else (1, 2, 3):
                near_copy(step, side).wait_recv()

    def activate(piece, tile):
        here = pl.ds(piece[0] * step_rows, len(piece) * step_rows)
        steps = pl.ds(piece[0], len(piece))
        cols = pl.ds(tile * unit_tile, unit_tile)
        row_count = len(piece) * step_rows
        pre_act = jnp.dot(dests[0, steps].reshape(row_count, width), up[:, cols], preferred_element_type=jnp.float32)
        hidden_grad = lax.dot_general(
            dests[1, steps].reshape(row_count, width), down[cols, :], (((1,), (1,)), ((), ())), preferred_element_type=jnp.float32
        )
        activated, pullback = jax.vjp(jax.nn.gelu, pre_act)
        hidden[here, cols] = activated.astype(jnp.bfloat16)
        pre_grad[here, cols] = pullback(hidden_grad)[0].astype(jnp.bfloat16)

    def project(piece, chunk):
        here = pl.ds(piece[0] * step_rows, len(piece) * step_rows)
        cols = columns(piece, chunk)
        part = lax.dot_general(
            pre_grad[here, :], up[cols, :], (((1,), (1,)), ((), ())), preferred_element_type=jnp.float32
        )
        for at in range(len(piece) * groups):
            step, group = piece[at // groups], at % groups
            parts[step, group, :, cols] = part[at * slots : (at + 1) * slots, :].astype(jnp.bfloat16)
        if piece in summed_twice:
            near = 1 + chunk
            part_copy(piece, chunk, 3, 1, near, 0).start()
            part_copy(piece, chunk, near, 0, near, 0).start()
        else:
            for side in (3, 1, 2):
                part_copy(piece, chunk, side, side - 1, side, 0).start()

    def relay_sum(piece, chunk):
        parts_landed(piece, chunk, pl.ds(0, 2), 0)
        here, cols = part_slice(piece, chunk)
        far = 2 - chunk
        total = parts[here, far, :, cols].astype(jnp.float32) + landed[here, 1, :, cols].astype(jnp.float32)
        parts[here, far, :, cols] = total.astype(jnp.bfloat16)
        part_copy(piece, chunk, far, 2, far, 1).start()

    def reduce(piece, chunk):
        cols = columns(piece, chunk)
        others = (0, 2) if piece in summed_twice else (0, 1, 2)
        if piece in summed_twice:
            parts_landed(piece, chunk, pl.ds(2, 1), 1)
        else:
            parts_landed(piece, chunk, pl.ds(0, 3), 0)
        for step in piece[::-1]:
            total = parts[step, 0, :, cols].astype(jnp.float32)
            for other in others:
                total = total + landed[step, other, :, cols].astype(jnp.float32)
            rounded = total.astype(jnp.bfloat16)
            if step == 0:
                back[0, :, cols] = rounded
            else:
                summed[step, :, cols] = rounded
                back_copy(step, cols).start()

    def weight_grad(which, other, out):
        tile = 512
        row_count = owners * step_rows

        def one(index, carry):
            cols = pl.ds(pl.multiple_of(index * tile, tile), tile)
            if which == 0:
                left, right = dests[0, :, :, :, cols].reshape(row_count, tile), other[...]
            else:
                left, right = other[:, cols], dests[1].reshape(row_count, width)
            term = lax.dot_general(left, right, (((0,), (0,)), ((), ())), preferred_element_type=jnp.float32)
            out[cols, :] = (term * scale).astype(jnp.bfloat16)
            return carry

        lax.fori_loop(0, out.shape[0] // tile, one, 0)

    out(1)
    out(4)
    out(5)
    arrive(0)
    out(2)
    out(3)
    arrive(1)
    forward(0)
    forward(1)
    arrive(2)
    arrive(3)
    out(6)
    out(7)
    for copy in weight_copies:
        copy.wait()
    gather(pieces[0])
    activate(pieces[0], 0)
    arrive(4)
    arrive(5)
    forward(2)
    forward(3)
    activate(pieces[0], 1)
    arrive(6)
    arrive(7)
    forward(4)
    forward(5)
    project(pieces[0], 0)
    project(pieces[0], 1)
    gather(pieces[1])
    activate(pieces[1], 0)
    forward(6)
    forward(7)
    activate(pieces[1], 1)
    project(pieces[1], 0)
    project(pieces[1], 1)
    gather(pieces[2])
    activate(pieces[2], 0)
    reduce(pieces[0], 0)
    reduce(pieces[0], 1)
    activate(pieces[2], 1)
    project(pieces[2], 0)
    project(pieces[2], 1)
    reduce(pieces[1], 0)
    reduce(pieces[1], 1)
    weight_grad(0, pre_grad, grad_up)
    reduce(pieces[2], 0)
    reduce(pieces[2], 1)
    weight_grad(1, hidden, grad_down)
    along_owner(back.at[1:owners], back.at[1:owners], 1, d_sends.at[4], e_recv).wait_recv()
    sent = [(sources.at[:, 1:owners], a_send), (dests.at[:, :, 1:3], d_sends.at[0])]
    if len(relayed) < owners:
        sent.append((dests.at[:, len(relayed) : owners, 3], d_sends.at[1]))
    sent += [(dests.at[:, 0 : len(relayed), 3], d_sends.at[2]), (landed, d_sends.at[3])]
    sent.append((back.at[1:owners], d_sends.at[4]))
    for whole, sem in sent:
        along_owner(whole, whole, 1, sem, sem).wait_send()


def fused(lang_ids, tokens, upstream, up_matrix, down_matrix, scale, owners, slots):
    width = tokens.shape[1]
    units = up_matrix.shape[1]
    groups = 4
    pieces = ((0, 1), (2, 3, 4, 5), (6, 7))
    chunk_counts = (2, 2, 2)
    total = owners * groups * slots
    vmem = pl.BlockSpec(memory_space=pltpu.VMEM)
    anywhere = pl.BlockSpec(memory_space=pltpu.HBM)
    dma = pltpu.SemaphoreType.DMA
    bf16 = jnp.bfloat16
    grid = (owners, groups, slots, width)
    held = [((total, units), bf16), ((total, units), bf16)]
    outs = [((owners, slots, width), bf16), ((owners * slots, tokens.shape[0]), bf16)]
    outs += [(tokens.shape, bf16), ((width, units), bf16), ((units, width), bf16)]
    both = jnp.concatenate([tokens, upstream], axis=0)
    back, placer, kept, grad_up, grad_down = pl.pallas_call(
        functools.partial(fused_kernel, owners, pieces, chunk_counts, scale),
        out_shape=[jax.ShapeDtypeStruct(*item) for item in outs],
        in_specs=[vmem] * 2 + [anywhere] * 2,
        out_specs=[vmem] * len(outs),
        scratch_shapes=[pltpu.VMEM(*item) for item in held]
        + [
            pltpu.VMEM((2, owners, slots, width), bf16),
            pltpu.VMEM((2,) + grid, bf16),
            pltpu.VMEM((width, units), bf16),
            pltpu.VMEM((units, width), bf16),
            pltpu.VMEM(grid, bf16),
            pltpu.VMEM((owners, groups - 1, slots, width), bf16),
            pltpu.VMEM((owners, slots, width), bf16),
            dma((2,)),
            dma,
            dma((owners - 1,)),
            dma((3, owners)),
            dma((2, len(pieces), max(chunk_counts))),
            dma((5,)),
            dma,
        ],
        compiler_params=pltpu.CompilerParams(
            collective_id=2, has_side_effects=True, vmem_limit_bytes=44 << 20
        ),
    )(lang_ids[None], both, up_matrix, down_matrix)
    return finish(placer, back, kept, grad_up, grad_down)


def finish_kernel(placer, back, upstream, up, down, input_grad, grad_up, grad_down, result, sem):
    splits = sem.shape[0] // 2
    copies = []
    for at, (source, dest) in enumerate(((up, grad_up), (down, grad_down))):
        size = source.shape[0] // splits
        for part in range(splits):
            here = pl.ds(part * size, size)
            copies.append(pltpu.make_async_copy(source.at[here], dest.at[here], sem.at[at * splits + part]))
            copies[-1].start()
    returned = jnp.concatenate([back[step].astype(jnp.float32) for step in range(back.shape[0])], axis=0)
    adapter_grad = lax.dot_general(
        placer[...], returned.astype(jnp.bfloat16), (((0,), (0,)), ((), ())), preferred_element_type=jnp.float32
    ).astype(jnp.bfloat16)
    result[...] = (upstream[...].astype(jnp.float32) + adapter_grad.astype(jnp.float32)).astype(jnp.bfloat16)
    pltpu.sync_copy(result, input_grad)
    for copy in copies:
        copy.wait()


def finish(placer, back, upstream, grad_up, grad_down):
    shape = upstream.shape
    anywhere = pl.BlockSpec(memory_space=pl.ANY)
    outs = [(shape, upstream.dtype), (grad_up.shape, upstream.dtype), (grad_down.shape, upstream.dtype)]
    return pl.pallas_call(
        finish_kernel,
        out_shape=[jax.ShapeDtypeStruct(*item) for item in outs],
        in_specs=[pl.BlockSpec(memory_space=pltpu.VMEM)] * 5,
        out_specs=[anywhere] * 3,
        scratch_shapes=[pltpu.VMEM(shape, upstream.dtype), pltpu.SemaphoreType.DMA((8,))],
        compiler_params=pltpu.CompilerParams(vmem_limit_bytes=16 << 20),
    )(placer, back, upstream, grad_up, grad_down)


def placement_matrix(block_ids, owners, slot_count):
    tok_count = block_ids.shape[0]
    matches = block_ids[:, None] == block_ids[None, :]
    positions = jnp.arange(tok_count, dtype=jnp.int32)
    earlier = positions[None, :] < positions[:, None]
    slots = jnp.sum(jnp.logical_and(matches, earlier), axis=1)
    target = block_ids * slot_count + slots
    return (target[None, :] == jnp.arange(owners * slot_count, dtype=jnp.int32)[:, None]).astype(
        jnp.bfloat16
    )


def local(tokens, upstream, lang_ids, up_weight, down_weight):
    owners = lax.axis_size("owner")
    groups = lax.axis_size("dp")
    tok_count, width = tokens.shape
    slots = max(2, 4 * tok_count // (3 * owners))
    rows_here = owners * slots
    up_matrix = up_weight[0]
    down_matrix = down_weight[0]
    grad_scale = float(tok_count * groups) ** (-0.5)
    one_kernel = (
        groups == 4
        and slots == 8
        and owners == 8
        and width % 512 == 0
        and up_matrix.shape[1] % 512 == 0
    )
    if one_kernel:
        input_grad, grad_up, grad_down = fused(
            lang_ids, tokens, upstream, up_matrix, down_matrix, grad_scale, owners, slots
        )
        return (input_grad, grad_up[None], grad_down[None])
    placer = placement_matrix(lang_ids, owners, slots)
    send_inputs = jnp.dot(placer, tokens, preferred_element_type=jnp.float32).astype(jnp.bfloat16)
    send_upstream = jnp.dot(placer, upstream, preferred_element_type=jnp.float32).astype(jnp.bfloat16)
    send_inputs = send_inputs.reshape(owners, slots, width)
    send_upstream = send_upstream.reshape(owners, slots, width)
    row_inputs, row_upstream = spread(
        send_inputs,
        send_upstream,
        owners,
        groups,
    )
    row_inputs = row_inputs.reshape(groups * rows_here, width)
    row_upstream = row_upstream.reshape(groups * rows_here, width)
    pre_act = jnp.dot(row_inputs, up_matrix, preferred_element_type=jnp.float32)
    activated, pullback = jax.vjp(jax.nn.gelu, pre_act)
    hidden = activated.astype(jnp.bfloat16)
    hidden_grad = lax.dot_general(
        row_upstream, down_matrix, (((1,), (1,)), ((), ())), preferred_element_type=jnp.float32
    )
    pre_grad = pullback(hidden_grad)[0].astype(jnp.bfloat16)
    parts = lax.dot_general(
        pre_grad, up_matrix, (((1,), (1,)), ((), ())), preferred_element_type=jnp.float32
    ).astype(jnp.bfloat16)
    returned = collect(parts.reshape(groups, owners, slots, width), owners, groups)
    up_term = lax.dot_general(
        row_inputs, pre_grad, (((0,), (0,)), ((), ())), preferred_element_type=jnp.float32
    )
    down_term = lax.dot_general(
        hidden, row_upstream, (((0,), (0,)), ((), ())), preferred_element_type=jnp.float32
    )
    grad_up = (up_term * grad_scale).astype(jnp.bfloat16)
    grad_down = (down_term * grad_scale).astype(jnp.bfloat16)
    adapter_grad = lax.dot_general(
        placer,
        returned.reshape(rows_here, width),
        (((0,), (0,)), ((), ())),
        preferred_element_type=jnp.float32,
    )
    input_grad = (upstream.astype(jnp.float32) + adapter_grad).astype(jnp.bfloat16)
    return (input_grad, grad_up[None], grad_down[None])


def solution(mesh):
    in_specs = (
        P(("owner", "dp"), None),
        P(("owner", "dp"), None),
        P(("owner", "dp")),
        P("owner", None, "dp"),
        P("owner", "dp", None),
    )
    out_specs = (P(("owner", "dp"), None), P("owner", None, "dp"), P("owner", "dp", None))
    return jax.shard_map(local, mesh=mesh, in_specs=in_specs, out_specs=out_specs, check_vma=False)
```

```python
import functools

import jax
import jax.numpy as jnp
from jax import lax
from jax.experimental import pallas as pl
from jax.experimental.pallas import tpu as pltpu
from jax.sharding import PartitionSpec as P

MESH = pl.DeviceIdType.MESH


def partner(index, step, count):
    total, bit = 0, 1
    while bit < count:
        digit = (index // bit) % 2
        total = total + bit * ((1 - digit) if (step // bit) % 2 else digit)
        bit *= 2
    return total


def greet(me_owner, me_group, owners, groups):
    barrier = pltpu.get_barrier_semaphore()
    for step in range(1, owners):
        pl.semaphore_signal(
            barrier, inc=1, device_id=(partner(me_owner, step, owners), me_group), device_id_type=MESH
        )
    for step in range(1, groups):
        pl.semaphore_signal(
            barrier, inc=1, device_id=(me_owner, partner(me_group, step, groups)), device_id_type=MESH
        )


def enter(me_owner, me_group, owners, groups):
    greet(me_owner, me_group, owners, groups)
    pl.semaphore_wait(pltpu.get_barrier_semaphore(), owners + groups - 2)


def spread_kernel(owners, groups, pieces, *refs):
    sources, dests = refs[0:2], refs[2:4]
    a_send, a_recv, b_send, b_recv, c_send, c_recv = refs[4:]
    me_owner, me_group = lax.axis_index("owner"), lax.axis_index("dp")
    per_piece = owners // pieces
    relay = groups == 4
    direct = [1, 2] if relay else list(range(1, groups))
    enter(me_owner, me_group, owners, groups)
    sends = []

    for step in range(1, owners):
        peer = partner(me_owner, step, owners)
        for which in range(2):
            copy = pltpu.make_async_remote_copy(
                src_ref=sources[which].at[peer],
                dst_ref=dests[which].at[me_group, me_owner],
                send_sem=a_send.at[which, step],
                recv_sem=a_recv.at[which, step],
                device_id=(peer, me_group),
                device_id_type=MESH,
            )
            copy.start()
            sends.append(copy)
    for which in range(2):
        dests[which][me_group, me_owner] = sources[which][me_owner]

    def piece_of(group, piece):
        here = partner(me_owner // per_piece, piece, pieces) * per_piece
        return group, pl.ds(here, per_piece)

    def hop(which, group, piece, step, send_sem, recv_sem):
        group_at, rows_at = piece_of(group, piece)
        return pltpu.make_async_remote_copy(
            src_ref=dests[which].at[group_at, rows_at],
            dst_ref=dests[which].at[group_at, rows_at],
            send_sem=send_sem,
            recv_sem=recv_sem,
            device_id=(me_owner, partner(me_group, step, groups)),
            device_id_type=MESH,
        )

    def forward(piece):
        for which in range(2):
            near, far = (1, 2) if which == 0 else (2, 1)
            group = partner(me_group, near, groups)
            hop(which, group, piece, near, b_send.at[which, near, piece], b_recv.at[which, near, piece]).wait_recv()
            copy = hop(which, group, piece, far, c_send.at[which, piece], c_recv.at[which, piece])
            copy.start()
            sends.append(copy)

    for piece in range(pieces):
        for inner in range(per_piece):
            step = piece * per_piece + inner
            if step == 0:
                continue
            peer = partner(me_owner, step, owners)
            for which in range(2):
                pltpu.make_async_remote_copy(
                    src_ref=sources[which].at[peer],
                    dst_ref=dests[which].at[me_group, peer],
                    send_sem=a_send.at[which, step],
                    recv_sem=a_recv.at[which, step],
                    device_id=(peer, me_group),
                    device_id_type=MESH,
                ).wait_recv()
        for step in direct:
            for which in range(2):
                copy = hop(which, me_group, piece, step, b_send.at[which, step, piece], b_recv.at[which, step, piece])
                copy.start()
                sends.append(copy)
        if relay and piece >= 1:
            forward(piece - 1)
    if relay:
        forward(pieces - 1)
    for piece in range(pieces):
        for which in range(2):
            for step in direct:
                if relay and step == (1 if which == 0 else 2):
                    continue
                group = partner(me_group, step, groups)
                hop(which, group, piece, step, b_send.at[which, step, piece], b_recv.at[which, step, piece]).wait_recv()
            if relay:
                group = partner(me_group, 3, groups)
                hop(which, group, piece, 1 if which else 2, c_send.at[which, piece], c_recv.at[which, piece]).wait_recv()
    for copy in sends:
        copy.wait_send()


def collect_kernel(owners, groups, pieces, parts, back, landed, summed, b_send, b_recv, a_send, a_recv):
    me_owner, me_group = lax.axis_index("owner"), lax.axis_index("dp")
    per_piece = owners // pieces
    enter(me_owner, me_group, owners, groups)
    sends = []

    def share(piece, step):
        here = pl.ds(partner(me_owner // per_piece, piece, pieces) * per_piece, per_piece)
        peer = partner(me_group, step, groups)
        return pltpu.make_async_remote_copy(
            src_ref=parts.at[peer, here],
            dst_ref=landed.at[step - 1, here],
            send_sem=b_send.at[step, piece],
            recv_sem=b_recv.at[step, piece],
            device_id=(me_owner, peer),
            device_id_type=MESH,
        )

    order = list(range(pieces))[::-1]
    for piece in order:
        for step in list(range(1, groups))[::-1]:
            copy = share(piece, step)
            copy.start()
            sends.append(copy)

    def ship(step):
        peer = partner(me_owner, step, owners)
        return pltpu.make_async_remote_copy(
            src_ref=summed.at[peer],
            dst_ref=back.at[me_owner],
            send_sem=a_send.at[step],
            recv_sem=a_recv.at[step],
            device_id=(peer, me_group),
            device_id_type=MESH,
        )

    for piece in order:
        for step in range(1, groups):
            share(piece, step).wait_recv()
        for inner in range(per_piece):
            step = piece * per_piece + inner
            peer = partner(me_owner, step, owners)
            total = parts[me_group, peer].astype(jnp.float32)
            for other in range(1, groups):
                total = total + landed[other - 1, peer].astype(jnp.float32)
            rounded = total.astype(jnp.bfloat16)
            if step == 0:
                back[peer] = rounded
            else:
                summed[peer] = rounded
                copy = ship(step)
                copy.start()
                sends.append(copy)
    for step in range(1, owners):
        peer = partner(me_owner, step, owners)
        pltpu.make_async_remote_copy(
            src_ref=summed.at[peer],
            dst_ref=back.at[peer],
            send_sem=a_send.at[step],
            recv_sem=a_recv.at[step],
            device_id=(peer, me_group),
            device_id_type=MESH,
        ).wait_recv()
    for copy in sends:
        copy.wait_send()


def spread(send_inputs, send_upstream, owners, groups):
    _, slots, width = send_inputs.shape
    pieces = owners // 2 if groups == 4 else 1
    whole = jax.ShapeDtypeStruct((groups, owners, slots, width), jnp.bfloat16)
    vmem = pl.BlockSpec(memory_space=pltpu.VMEM)
    dma = pltpu.SemaphoreType.DMA
    return pl.pallas_call(
        functools.partial(spread_kernel, owners, groups, pieces),
        out_shape=(whole, whole),
        in_specs=[vmem, vmem],
        out_specs=(vmem, vmem),
        scratch_shapes=[
            dma((2, owners)),
            dma((2, owners)),
            dma((2, groups, pieces)),
            dma((2, groups, pieces)),
            dma((2, pieces)),
            dma((2, pieces)),
        ],
        compiler_params=pltpu.CompilerParams(
            collective_id=0, has_side_effects=True, vmem_limit_bytes=24 << 20
        ),
    )(send_inputs, send_upstream)


def collect(parts, owners, groups):
    _, _, slots, width = parts.shape
    pieces = owners // 2 if groups == 4 else 1
    vmem = pl.BlockSpec(memory_space=pltpu.VMEM)
    dma = pltpu.SemaphoreType.DMA
    return pl.pallas_call(
        functools.partial(collect_kernel, owners, groups, pieces),
        out_shape=jax.ShapeDtypeStruct((owners, slots, width), jnp.bfloat16),
        in_specs=[vmem],
        out_specs=vmem,
        scratch_shapes=[
            pltpu.VMEM((groups - 1, owners, slots, width), jnp.bfloat16),
            pltpu.VMEM((owners, slots, width), jnp.bfloat16),
            dma((groups, pieces)),
            dma((groups, pieces)),
            dma((owners,)),
            dma((owners,)),
        ],
        compiler_params=pltpu.CompilerParams(
            collective_id=1, has_side_effects=True, vmem_limit_bytes=24 << 20
        ),
    )(parts)


def fused_kernel(owners, pieces, chunk_counts, scale, *refs):
    (ids, arrivals, up_hbm, down_hbm), refs = refs[0:4], refs[4:]
    tok_count = ids.shape[1]
    (back, placer_out, kept, grad_up, grad_down), refs = refs[0:5], refs[5:]
    (hidden, pre_grad), refs = refs[0:2], refs[2:]
    sources, dests, up, down, parts, landed, summed = refs[0:7]
    w_sem, a_send, a_recv, b_recv, c_recv, d_sends, e_recv = refs[7:]
    groups = 4
    slots, width = sources.shape[2:]
    units = up.shape[1]
    step_rows = groups * slots
    relayed = tuple(range(8))
    summed_twice = pieces[0:0]
    unit_tile = units // 2
    me_owner, me_group = lax.axis_index("owner"), lax.axis_index("dp")
    greet(me_owner, me_group, owners, groups)
    weight_copies = [
        pltpu.make_async_copy(up_hbm, up, w_sem.at[0]),
        pltpu.make_async_copy(down_hbm, down, w_sem.at[1]),
    ]
    row_ids = ids[...]
    square = (tok_count, tok_count)
    first_at = lax.broadcasted_iota(jnp.int32, square, 0)
    second_at = lax.broadcasted_iota(jnp.int32, square, 1)
    spread_ids = jnp.broadcast_to(row_ids.astype(jnp.float32), square)
    column_ids = jnp.sum(jnp.where(first_at == second_at, spread_ids, 0.0), axis=1, keepdims=True)
    same = jnp.logical_and(column_ids == spread_ids, first_at < second_at)
    ranks = jnp.sum(jnp.where(same, 1.0, 0.0), axis=0, keepdims=True).astype(jnp.int32)
    target = jnp.bitwise_xor(row_ids, me_owner) * slots + ranks
    positions = lax.broadcasted_iota(jnp.int32, (owners * slots, tok_count), 0)
    placer = jnp.where(positions == target, 1.0, 0.0).astype(jnp.bfloat16)
    placer_out[...] = placer
    kept[...] = arrivals[tok_count : 2 * tok_count, :]
    for which in range(2):
        placed = jnp.dot(placer, arrivals[which * tok_count : (which + 1) * tok_count, :], preferred_element_type=jnp.float32)
        for step in range(owners):
            block = placed[step * slots : (step + 1) * slots, :].astype(jnp.bfloat16)
            (sources if step else dests)[(which, step) if step else (which, 0, 0)] = block
    pl.semaphore_wait(pltpu.get_barrier_semaphore(), owners + groups - 2)

    def along_owner(source, dest, step, send_sem, recv_sem):
        return pltpu.make_async_remote_copy(
            src_ref=source,
            dst_ref=dest,
            send_sem=send_sem,
            recv_sem=recv_sem,
            device_id=(partner(me_owner, step, owners), me_group),
            device_id_type=MESH,
        )

    def along_group(source, dest, step, send_sem, recv_sem):
        return pltpu.make_async_remote_copy(
            src_ref=source,
            dst_ref=dest,
            send_sem=send_sem,
            recv_sem=recv_sem,
            device_id=(me_owner, partner(me_group, step, groups)),
            device_id_type=MESH,
        )

    def out_copy(step):
        return along_owner(sources.at[:, step], dests.at[:, step, 0], step, a_send, a_recv.at[step - 1])

    def near_copy(step, side):
        return along_group(
            dests.at[:, step, 0], dests.at[:, step, side], side, d_sends.at[0 if side < 3 else 1], b_recv.at[side - 1, step]
        )

    def relay_copy(which, step):
        first, second = (1, 2) if which == 0 else (2, 1)
        return along_group(
            dests.at[which, step, first], dests.at[which, step, 3], second, d_sends.at[2], b_recv.at[2, step]
        )

    def columns(piece, chunk):
        size = width // chunk_counts[pieces.index(piece)]
        return pl.ds(chunk * size, size)

    def part_slice(piece, chunk):
        return pl.ds(piece[0], len(piece)), columns(piece, chunk)

    def part_copy(piece, chunk, side, slot, towards, leg):
        here, cols = part_slice(piece, chunk)
        return along_group(
            parts.at[here, side, :, cols],
            landed.at[here, slot, :, cols],
            towards,
            d_sends.at[3],
            c_recv.at[leg, pieces.index(piece), chunk],
        )

    def parts_landed(piece, chunk, slots_in, leg):
        here, cols = part_slice(piece, chunk)
        whole = landed.at[here, slots_in, :, cols]
        along_group(whole, whole, 1, d_sends.at[3], c_recv.at[leg, pieces.index(piece), chunk]).wait_recv()

    def back_copy(step, cols):
        return along_owner(summed.at[step, :, cols], back.at[step, :, cols], step, d_sends.at[4], e_recv)

    def out(*steps):
        for step in steps:
            out_copy(step).start()

    def arrive(*steps):
        for step in steps:
            if step:
                out_copy(step).wait_recv()
            for side in (1, 2) if step in relayed else (3, 1, 2):
                near_copy(step, side).start()

    def forward(*steps):
        for step in steps:
            for side in (1, 2):
                near_copy(step, side).wait_recv()
            for which in range(2):
                relay_copy(which, step).start()

    def gather(piece):
        for step in piece:
            for side in (3,) if step in relayed else (1, 2, 3):
                near_copy(step, side).wait_recv()

    def activate(piece, tile):
        here = pl.ds(piece[0] * step_rows, len(piece) * step_rows)
        steps = pl.ds(piece[0], len(piece))
        cols = pl.ds(tile * unit_tile, unit_tile)
        row_count = len(piece) * step_rows
        pre_act = jnp.dot(dests[0, steps].reshape(row_count, width), up[:, cols], preferred_element_type=jnp.float32)
        hidden_grad = lax.dot_general(
            dests[1, steps].reshape(row_count, width), down[cols, :], (((1,), (1,)), ((), ())), preferred_element_type=jnp.float32
        )
        activated, pullback = jax.vjp(jax.nn.gelu, pre_act)
        hidden[here, cols] = activated.astype(jnp.bfloat16)
        pre_grad[here, cols] = pullback(hidden_grad)[0].astype(jnp.bfloat16)

    def project(piece, chunk):
        here = pl.ds(piece[0] * step_rows, len(piece) * step_rows)
        cols = columns(piece, chunk)
        part = lax.dot_general(
            pre_grad[here, :], up[cols, :], (((1,), (1,)), ((), ())), preferred_element_type=jnp.float32
        )
        for at in range(len(piece) * groups):
            step, group = piece[at // groups], at % groups
            parts[step, group, :, cols] = part[at * slots : (at + 1) * slots, :].astype(jnp.bfloat16)
        if piece in summed_twice:
            near = 1 + chunk
            part_copy(piece, chunk, 3, 1, near, 0).start()
            part_copy(piece, chunk, near, 0, near, 0).start()
        else:
            for side in (3, 1, 2):
                part_copy(piece, chunk, side, side - 1, side, 0).start()

    def relay_sum(piece, chunk):
        parts_landed(piece, chunk, pl.ds(0, 2), 0)
        here, cols = part_slice(piece, chunk)
        far = 2 - chunk
        total = parts[here, far, :, cols].astype(jnp.float32) + landed[here, 1, :, cols].astype(jnp.float32)
        parts[here, far, :, cols] = total.astype(jnp.bfloat16)
        part_copy(piece, chunk, far, 2, far, 1).start()

    def reduce(piece, chunk):
        cols = columns(piece, chunk)
        others = (0, 2) if piece in summed_twice else (0, 1, 2)
        if piece in summed_twice:
            parts_landed(piece, chunk, pl.ds(2, 1), 1)
        else:
            parts_landed(piece, chunk, pl.ds(0, 3), 0)
        for step in piece[::-1]:
            total = parts[step, 0, :, cols].astype(jnp.float32)
            for other in others:
                total = total + landed[step, other, :, cols].astype(jnp.float32)
            rounded = total.astype(jnp.bfloat16)
            if step == 0:
                back[0, :, cols] = rounded
            else:
                summed[step, :, cols] = rounded
                back_copy(step, cols).start()

    def weight_grad(which, other, out):
        tile = 512
        row_count = owners * step_rows

        def one(index, carry):
            cols = pl.ds(pl.multiple_of(index * tile, tile), tile)
            if which == 0:
                left, right = dests[0, :, :, :, cols].reshape(row_count, tile), other[...]
            else:
                left, right = other[:, cols], dests[1].reshape(row_count, width)
            term = lax.dot_general(left, right, (((0,), (0,)), ((), ())), preferred_element_type=jnp.float32)
            out[cols, :] = (term * scale).astype(jnp.bfloat16)
            return carry

        lax.fori_loop(0, out.shape[0] // tile, one, 0)

    out(1)
    out(4)
    out(5)
    arrive(0)
    for copy in weight_copies:
        copy.start()
    out(2)
    out(3)
    arrive(1)
    forward(0)
    forward(1)
    arrive(2)
    arrive(3)
    out(6)
    out(7)
    for copy in weight_copies:
        copy.wait()
    gather(pieces[0])
    activate(pieces[0], 0)
    arrive(4)
    arrive(5)
    forward(2)
    forward(3)
    activate(pieces[0], 1)
    arrive(6)
    arrive(7)
    forward(4)
    forward(5)
    project(pieces[0], 0)
    project(pieces[0], 1)
    gather(pieces[1])
    activate(pieces[1], 0)
    forward(6)
    forward(7)
    activate(pieces[1], 1)
    project(pieces[1], 0)
    project(pieces[1], 1)
    gather(pieces[2])
    activate(pieces[2], 0)
    reduce(pieces[0], 0)
    reduce(pieces[0], 1)
    activate(pieces[2], 1)
    project(pieces[2], 0)
    project(pieces[2], 1)
    reduce(pieces[1], 0)
    reduce(pieces[1], 1)
    weight_grad(0, pre_grad, grad_up)
    reduce(pieces[2], 0)
    reduce(pieces[2], 1)
    weight_grad(1, hidden, grad_down)
    along_owner(back.at[1:owners], back.at[1:owners], 1, d_sends.at[4], e_recv).wait_recv()
    sent = [(sources.at[:, 1:owners], a_send), (dests.at[:, :, 1:3], d_sends.at[0])]
    if len(relayed) < owners:
        sent.append((dests.at[:, len(relayed) : owners, 3], d_sends.at[1]))
    sent += [(dests.at[:, 0 : len(relayed), 3], d_sends.at[2]), (landed, d_sends.at[3])]
    sent.append((back.at[1:owners], d_sends.at[4]))
    for whole, sem in sent:
        along_owner(whole, whole, 1, sem, sem).wait_send()


def fused(lang_ids, tokens, upstream, up_matrix, down_matrix, scale, owners, slots):
    width = tokens.shape[1]
    units = up_matrix.shape[1]
    groups = 4
    pieces = ((0, 1), (2, 3, 4, 5), (6, 7))
    chunk_counts = (2, 2, 2)
    total = owners * groups * slots
    vmem = pl.BlockSpec(memory_space=pltpu.VMEM)
    anywhere = pl.BlockSpec(memory_space=pltpu.HBM)
    dma = pltpu.SemaphoreType.DMA
    bf16 = jnp.bfloat16
    grid = (owners, groups, slots, width)
    held = [((total, units), bf16), ((total, units), bf16)]
    outs = [((owners, slots, width), bf16), ((owners * slots, tokens.shape[0]), bf16)]
    outs += [(tokens.shape, bf16), ((width, units), bf16), ((units, width), bf16)]
    both = jnp.concatenate([tokens, upstream], axis=0)
    back, placer, kept, grad_up, grad_down = pl.pallas_call(
        functools.partial(fused_kernel, owners, pieces, chunk_counts, scale),
        out_shape=[jax.ShapeDtypeStruct(*item) for item in outs],
        in_specs=[vmem] * 2 + [anywhere] * 2,
        out_specs=[vmem] * len(outs),
        scratch_shapes=[pltpu.VMEM(*item) for item in held]
        + [
            pltpu.VMEM((2, owners, slots, width), bf16),
            pltpu.VMEM((2,) + grid, bf16),
            pltpu.VMEM((width, units), bf16),
            pltpu.VMEM((units, width), bf16),
            pltpu.VMEM(grid, bf16),
            pltpu.VMEM((owners, groups - 1, slots, width), bf16),
            pltpu.VMEM((owners, slots, width), bf16),
            dma((2,)),
            dma,
            dma((owners - 1,)),
            dma((3, owners)),
            dma((2, len(pieces), max(chunk_counts))),
            dma((5,)),
            dma,
        ],
        compiler_params=pltpu.CompilerParams(
            collective_id=2, has_side_effects=True, vmem_limit_bytes=44 << 20
        ),
    )(lang_ids[None], both, up_matrix, down_matrix)
    return finish(placer, back, kept, grad_up, grad_down)


def finish_kernel(placer, back, upstream, up, down, input_grad, grad_up, grad_down, result, sem):
    splits = sem.shape[0] // 2
    copies = []
    for at, (source, dest) in enumerate(((up, grad_up), (down, grad_down))):
        size = source.shape[0] // splits
        for part in range(splits):
            here = pl.ds(part * size, size)
            copies.append(pltpu.make_async_copy(source.at[here], dest.at[here], sem.at[at * splits + part]))
            copies[-1].start()
    returned = jnp.concatenate([back[step].astype(jnp.float32) for step in range(back.shape[0])], axis=0)
    adapter_grad = lax.dot_general(
        placer[...], returned.astype(jnp.bfloat16), (((0,), (0,)), ((), ())), preferred_element_type=jnp.float32
    ).astype(jnp.bfloat16)
    result[...] = (upstream[...].astype(jnp.float32) + adapter_grad.astype(jnp.float32)).astype(jnp.bfloat16)
    pltpu.sync_copy(result, input_grad)
    for copy in copies:
        copy.wait()


def finish(placer, back, upstream, grad_up, grad_down):
    shape = upstream.shape
    anywhere = pl.BlockSpec(memory_space=pl.ANY)
    outs = [(shape, upstream.dtype), (grad_up.shape, upstream.dtype), (grad_down.shape, upstream.dtype)]
    return pl.pallas_call(
        finish_kernel,
        out_shape=[jax.ShapeDtypeStruct(*item) for item in outs],
        in_specs=[pl.BlockSpec(memory_space=pltpu.VMEM)] * 5,
        out_specs=[anywhere] * 3,
        scratch_shapes=[pltpu.VMEM(shape, upstream.dtype), pltpu.SemaphoreType.DMA((8,))],
        compiler_params=pltpu.CompilerParams(vmem_limit_bytes=16 << 20),
    )(placer, back, upstream, grad_up, grad_down)


def placement_matrix(block_ids, owners, slot_count):
    tok_count = block_ids.shape[0]
    matches = block_ids[:, None] == block_ids[None, :]
    positions = jnp.arange(tok_count, dtype=jnp.int32)
    earlier = positions[None, :] < positions[:, None]
    slots = jnp.sum(jnp.logical_and(matches, earlier), axis=1)
    target = block_ids * slot_count + slots
    return (target[None, :] == jnp.arange(owners * slot_count, dtype=jnp.int32)[:, None]).astype(
        jnp.bfloat16
    )


def local(tokens, upstream, lang_ids, up_weight, down_weight):
    owners = lax.axis_size("owner")
    groups = lax.axis_size("dp")
    tok_count, width = tokens.shape
    slots = max(2, 4 * tok_count // (3 * owners))
    rows_here = owners * slots
    up_matrix = up_weight[0]
    down_matrix = down_weight[0]
    grad_scale = float(tok_count * groups) ** (-0.5)
    one_kernel = (
        groups == 4
        and slots == 8
        and owners == 8
        and width % 512 == 0
        and up_matrix.shape[1] % 512 == 0
    )
    if one_kernel:
        input_grad, grad_up, grad_down = fused(
            lang_ids, tokens, upstream, up_matrix, down_matrix, grad_scale, owners, slots
        )
        return (input_grad, grad_up[None], grad_down[None])
    placer = placement_matrix(lang_ids, owners, slots)
    send_inputs = jnp.dot(placer, tokens, preferred_element_type=jnp.float32).astype(jnp.bfloat16)
    send_upstream = jnp.dot(placer, upstream, preferred_element_type=jnp.float32).astype(jnp.bfloat16)
    send_inputs = send_inputs.reshape(owners, slots, width)
    send_upstream = send_upstream.reshape(owners, slots, width)
    row_inputs, row_upstream = spread(
        send_inputs,
        send_upstream,
        owners,
        groups,
    )
    row_inputs = row_inputs.reshape(groups * rows_here, width)
    row_upstream = row_upstream.reshape(groups * rows_here, width)
    pre_act = jnp.dot(row_inputs, up_matrix, preferred_element_type=jnp.float32)
    activated, pullback = jax.vjp(jax.nn.gelu, pre_act)
    hidden = activated.astype(jnp.bfloat16)
    hidden_grad = lax.dot_general(
        row_upstream, down_matrix, (((1,), (1,)), ((), ())), preferred_element_type=jnp.float32
    )
    pre_grad = pullback(hidden_grad)[0].astype(jnp.bfloat16)
    parts = lax.dot_general(
        pre_grad, up_matrix, (((1,), (1,)), ((), ())), preferred_element_type=jnp.float32
    ).astype(jnp.bfloat16)
    returned = collect(parts.reshape(groups, owners, slots, width), owners, groups)
    up_term = lax.dot_general(
        row_inputs, pre_grad, (((0,), (0,)), ((), ())), preferred_element_type=jnp.float32
    )
    down_term = lax.dot_general(
        hidden, row_upstream, (((0,), (0,)), ((), ())), preferred_element_type=jnp.float32
    )
    grad_up = (up_term * grad_scale).astype(jnp.bfloat16)
    grad_down = (down_term * grad_scale).astype(jnp.bfloat16)
    adapter_grad = lax.dot_general(
        placer,
        returned.reshape(rows_here, width),
        (((0,), (0,)), ((), ())),
        preferred_element_type=jnp.float32,
    )
    input_grad = (upstream.astype(jnp.float32) + adapter_grad).astype(jnp.bfloat16)
    return (input_grad, grad_up[None], grad_down[None])


def solution(mesh):
    in_specs = (
        P(("owner", "dp"), None),
        P(("owner", "dp"), None),
        P(("owner", "dp")),
        P("owner", None, "dp"),
        P("owner", "dp", None),
    )
    out_specs = (P(("owner", "dp"), None), P("owner", None, "dp"), P("owner", "dp", None))
    return jax.shard_map(local, mesh=mesh, in_specs=in_specs, out_specs=out_specs, check_vma=False)
```
